32 devices in a mesh: feat: 4 (over x, core), rows: 8 (over z, y).
Axes of the slice: x: 2, y: 2, z: 4, core: 2. Of those that a mesh axis runs over, the one named last changes fastest.
Arguments:
- acts: bfloat16 [8192, 16384], P('rows', 'feat'), may hold values from -6 to 6
- grads_out: bfloat16 [8192, 16384], P('rows', 'feat'), may hold values from -0.59765625 to 0.59765625
- proj_in: bfloat16 [16384, 128], P('feat'), may hold values from -0.046875 to 0.046875
- proj_out: bfloat16 [16384, 128], P('feat'), may hold values from -0.046875 to 0.046875
- doc_ids: int32 [8192], P('rows'), may hold values from -1 to 31, as said below
- block_counts: int32 [32], replicated, may hold values from 1 to 17, as said below
- inverse_dense: bfloat16 [16384, 16384], P('rows', 'feat'), may hold values from -0.046875 to 0.046875
- inverse_diag: float32 [16384], P('rows'), may hold values from 0.5 to 2
- train_grads: bfloat16 [4096, 16384], P('rows', 'feat'), may hold values from -0.046875 to 0.046875
Outputs:
- scores: float32 [32, 4096], P('feat', 'rows')
The draws below stay inside these ranges and needn't reach their ends.
Inputs may be any that keep to these rules, and one draw needn't show every extreme that they name: `doc_ids`: documents are laid end to end in order, document d over block_counts_d whole blocks of 128 tokens; its tokens come first and the rest of its last block is padding with id -1; every block holds real tokens of its document. `block_counts`: the counts sum to 64; one document has exactly the most.
All inputs are finite; a program needn't handle non-finite values.
Results may differ from the reference program's by a relative error of at most 0.0057.
Values may be sent and summed in bfloat16 or wider, within the bound.
No kernel may reach another device: no remote copies, remote signals or barrier semaphores. Data moves between devices by JAX's collectives and lax.ppermute only.
A program may use at most 128 MiB of HBM per device.

```python
import math
import jax
import jax.numpy as jnp
from jax import lax

D = 16384
K = 128
BLOCK = 128
TOKENS = 8192
NBLK = 64
DOCS = 32
NTRAIN = 4096
F = 16384


def layout(key):
    base = jax.random.fold_in(key, 7)
    first, second, third = jax.random.split(base, 3)
    spare = NBLK - DOCS
    heavy = (spare + 1) // 2
    rest = spare - heavy
    chosen = jax.random.randint(third, (), 0, DOCS)
    picks = jax.random.randint(first, (max(rest, 1),), 0, DOCS - 1)
    picks = jnp.where(picks >= chosen, picks + 1, picks)
    valid = (jnp.arange(max(rest, 1), dtype=jnp.int32) < rest).astype(jnp.int32)
    docs_all = jnp.arange(DOCS, dtype=jnp.int32)
    spread = jnp.sum((picks[:, None] == docs_all[None, :]).astype(jnp.int32) * valid[:, None], axis=0)
    counts = 1 + spread + jnp.where(docs_all == chosen, heavy, 0)
    pads = jax.random.randint(second, (DOCS,), 0, BLOCK)
    return (counts.astype(jnp.int32), pads.astype(jnp.int32))


def draw_block_counts(key, part):
    counts, pads = layout(key)
    return counts


def draw_doc_ids(key, part):
    counts, pads = layout(key)
    starts = jnp.cumsum(counts) - counts
    places = jnp.arange(NBLK, dtype=jnp.int32)
    owner = jnp.sum((starts[None, :] <= places[:, None]).astype(jnp.int32), axis=1) - 1
    position = jnp.arange(TOKENS, dtype=jnp.int32)
    docs_here = owner[position // BLOCK]
    offset = position - starts[docs_here] * BLOCK
    length = counts[docs_here] * BLOCK - pads[docs_here]
    return jnp.where(offset < length, docs_here, -1).astype(jnp.int32)


def steps_of(key, dims, pieces, smallest, high):
    def one(axis_at, parts):
        draws = jax.random.uniform(jax.random.fold_in(jax.random.fold_in(key, 6), axis_at), (parts,), jnp.float32, smallest / len(pieces), high / len(pieces))
        return jnp.repeat(jnp.exp(draws), dims[axis_at] // parts).reshape((-1,) + (1,) * (len(dims) - axis_at - 1))

    factor_of = one(*pieces[0])
    for cut in pieces[1:]:
        factor_of = factor_of * one(*cut)
    return factor_of


def normal_values(stream_key, dims, scale, bound, pieces=(), held_as=jnp.bfloat16):
    result = scale * jax.random.normal(stream_key, dims, jnp.float32)
    if pieces:
        result = result * steps_of(stream_key, dims, pieces, -0.22, 0.18)
    return jnp.clip(result, -bound, bound).astype(held_as)


def setup_inputs(seed: int = 0) -> dict:
    key_list = jax.random.split(jax.random.key(seed), 10)
    return {
        "acts": normal_values(key_list[0], (TOKENS, D), 1.0, 6.0, ((0, 8), (1, 4))),
        "grads_out": normal_values(key_list[1], (TOKENS, D), 0.1, 0.59765625, ((0, 8), (1, 4))),
        "proj_in": normal_values(key_list[2], (D, K), D ** -0.5, 0.046875, ((0, 4),)),
        "proj_out": normal_values(key_list[3], (D, K), D ** -0.5, 0.046875, ((0, 4),)),
        "doc_ids": draw_doc_ids(jax.random.fold_in(key_list[9], 71), 0),
        "block_counts": draw_block_counts(jax.random.fold_in(key_list[9], 71), 0),
        "inverse_dense": normal_values(key_list[6], (F, F), F ** -0.5, 0.046875, ((0, 8), (1, 4))),
        "inverse_diag": jnp.clip(jnp.exp(math.log(2.0) - 1.3862944 * jax.random.uniform(key_list[7], (F,), jnp.float32) ** steps_of(key_list[7], (F,), ((0, 8),), -0.2, 0.2)), 0.5, 2.0),
        "train_grads": normal_values(key_list[8], (NTRAIN, F), F ** -0.5, 0.046875, ((0, 8), (1, 4))),
    }


def owners(block_counts):
    starts = jnp.cumsum(block_counts) - block_counts
    places = jnp.arange(NBLK, dtype=jnp.int32)
    return jnp.sum((starts[None, :] <= places[:, None]).astype(jnp.int32), axis=1) - 1


def reference(acts, grads_out, proj_in, proj_out, doc_ids, block_counts, inverse_dense, inverse_diag, train_grads):
    xin = jnp.dot(acts, proj_in, preferred_element_type=jnp.float32).astype(jnp.bfloat16)
    gout = jnp.dot(grads_out, proj_out, preferred_element_type=jnp.float32).astype(jnp.bfloat16)
    owner = owners(block_counts)
    tok_owner = jnp.repeat(owner, BLOCK)
    gmask = jnp.where((doc_ids == tok_owner)[:, None], gout, jnp.zeros_like(gout))
    left = gmask.astype(jnp.float32).reshape(NBLK, BLOCK, K)
    right = xin.astype(jnp.float32).reshape(NBLK, BLOCK, K)
    blocksum = jnp.einsum("kta,ktc->kac", left, right).reshape(NBLK, K * K)
    member = (owner[None, :] == jnp.arange(DOCS, dtype=jnp.int32)[:, None]).astype(jnp.float32)
    summed = jnp.dot(member, blocksum, precision=lax.Precision.HIGHEST)
    docgrad = (summed / block_counts.astype(jnp.float32)[:, None]).astype(jnp.bfloat16)
    dense = jnp.dot(docgrad, inverse_dense, preferred_element_type=jnp.float32)
    precond = (dense + docgrad.astype(jnp.float32) * inverse_diag[None, :]).astype(jnp.bfloat16)
    return jnp.dot(precond, train_grads.T, preferred_element_type=jnp.float32)
```

```python
import functools

import jax
import jax.numpy as jnp
from jax import lax
from jax.experimental import pallas as pl
from jax.experimental.pallas import tpu as pltpu
from jax.sharding import PartitionSpec as P

BLOCK = 128
LANES = 128


def swap(x, axis, mask):
    count = lax.axis_size(axis)
    return lax.ppermute(x, axis, [(i, i ^ mask) for i in range(count)])


def pick(x, index, axis=0):
    return lax.dynamic_index_in_dim(x, index, axis, keepdims=False)


def dense_kernel(half_ref, grad_ref, diag_ref, inverse_ref, out_ref):
    units, docs, _ = grad_ref.shape
    left = jnp.concatenate([grad_ref[a] for a in range(units)], axis=1)
    total = jnp.dot(left, inverse_ref[...], preferred_element_type=jnp.float32)
    out_ref[...] = total.astype(out_ref.dtype)
    wide = out_ref.shape[1] // LANES
    first = (half_ref[0] * pl.num_programs(0) + pl.program_id(0)) * wide - half_ref[1]
    for q in range(wide):
        unit = first + q

        @pl.when((unit >= 0) & (unit < units))
        def _():
            at = jnp.clip(unit, 0, units - 1)
            term = grad_ref[at].astype(jnp.float32) * diag_ref[pl.ds(at, 1), :]
            cols = slice(q * LANES, (q + 1) * LANES)
            out_ref[:, cols] = (total[:, cols] + term).astype(out_ref.dtype)


def dense_half(half, start, docgrad, diag, inverse, dtype):
    units, docs, _ = docgrad.shape
    depth, cols = inverse.shape
    wide = min(512, cols // 2)
    steps = cols // 2 // wide
    return pl.pallas_call(
        dense_kernel,
        out_shape=jax.ShapeDtypeStruct((docs, cols // 2), dtype),
        grid_spec=pltpu.PrefetchScalarGridSpec(
            num_scalar_prefetch=1,
            grid=(steps,),
            in_specs=[
                pl.BlockSpec((units, docs, LANES), lambda n, s: (0, 0, 0)),
                pl.BlockSpec((units, LANES), lambda n, s: (0, 0)),
                pl.BlockSpec((depth, wide), lambda n, s: (0, s[0] * steps + n)),
            ],
            out_specs=pl.BlockSpec((docs, wide), lambda n, s: (0, n)),
        ),
        compiler_params=pltpu.CompilerParams(vmem_limit_bytes=24 << 20),
    )(jnp.stack([half, start]).astype(jnp.int32), docgrad, diag, inverse)


def score_kernel(where_ref, own_ref, other_ref, train_ref, out_ref):
    chunks, few, _ = own_ref.shape

    def add(source_ref, fresh):
        left = jnp.concatenate([source_ref[k] for k in range(chunks)], axis=0)
        got = lax.dot_general(
            left, train_ref[...], (((1,), (1,)), ((), ())), preferred_element_type=jnp.float32
        )
        for k in range(chunks):
            at = where_ref[1] ^ k
            piece = got[k * few : (k + 1) * few]
            out_ref[at] = piece if fresh else out_ref[at] + piece

    @pl.when(pl.program_id(0) == 0)
    def _():
        add(own_ref, True)

    @pl.when(pl.program_id(0) == 1)
    def _():
        add(other_ref, False)


def score(side, place, own, other, train):
    chunks, few, half = own.shape
    count = train.shape[0]
    return pl.pallas_call(
        score_kernel,
        out_shape=jax.ShapeDtypeStruct((chunks, few, count), jnp.float32),
        grid_spec=pltpu.PrefetchScalarGridSpec(
            num_scalar_prefetch=1,
            grid=(2,),
            in_specs=[
                pl.BlockSpec((chunks, few, half), lambda n, s: (0, 0, 0)),
                pl.BlockSpec((chunks, few, half), lambda n, s: (0, 0, 0)),
                pl.BlockSpec((count, half), lambda n, s: (0, s[0] ^ n)),
            ],
            out_specs=pl.BlockSpec((chunks, few, count), lambda n, s: (0, 0, 0)),
        ),
        compiler_params=pltpu.CompilerParams(vmem_limit_bytes=24 << 20),
    )(jnp.stack([side, place]).astype(jnp.int32), own, other, train)


def per_device(
    acts,
    grads_out,
    proj_in,
    proj_out,
    doc_ids,
    block_counts,
    inverse_dense,
    inverse_diag,
    train_grads,
):
    tokens = acts.shape[0]
    rows = lax.axis_size("rows")
    feats = lax.axis_size("feat")
    row = lax.axis_index("rows")
    feat = lax.axis_index("feat")
    width = proj_in.shape[1]
    docs = block_counts.shape[0]
    part = tokens // feats
    mine = part // BLOCK
    f32, b16 = jnp.float32, jnp.bfloat16

    part_in = jnp.dot(acts, proj_in, preferred_element_type=f32)
    part_out = jnp.dot(grads_out, proj_out, preferred_element_type=f32)
    both = jnp.stack([part_in, part_out]).reshape(2, feats, part, width)
    mask = 1
    while mask < feats:
        left = both.reshape(2, both.shape[1] // 2, 2, part, width)
        bit = (feat // mask) % 2
        sent = pick(left, 1 - bit, 2).astype(f32 if mask == 1 else b16)
        both = pick(left, bit, 2) + swap(sent, "feat", mask).astype(f32)
        mask *= 2
    xin = both[0].reshape(mine, BLOCK, width).astype(b16)
    gout = both[1].reshape(mine, BLOCK, width).astype(b16)

    order = jnp.arange(docs, dtype=jnp.int32)
    starts = jnp.sum(jnp.where(order[None, :] < order[:, None], block_counts[None, :], 0), axis=1)
    ends = starts + block_counts
    blocks = tokens // BLOCK
    here = row * blocks + feat * mine + jnp.arange(mine, dtype=jnp.int32)
    owner = jnp.sum((starts[None, :] <= here[:, None]).astype(jnp.int32), axis=1) - 1
    ids = pick(doc_ids.reshape(feats, mine, BLOCK), feat)
    gmask = jnp.where((ids == owner[:, None])[:, :, None], gout, jnp.zeros_like(gout))
    sums = jnp.einsum("kta,ktc->kac", gmask, xin, preferred_element_type=f32).astype(b16)

    units = width // rows
    chips = feats // 2
    parts = sums.reshape(mine, rows, units, width).transpose(1, 0, 2, 3)
    parts = jnp.broadcast_to(parts[None], (chips,) + parts.shape).reshape(chips * rows, mine, units, width)
    groups = [[(2 * x + c) * rows + r for x in range(chips) for r in range(rows)] for c in range(2)]
    near = lax.all_to_all(parts, ("feat", "rows"), 0, 0, tiled=True, axis_index_groups=groups)
    far = swap(near, "feat", 1)
    core = feat % 2
    shape = (2, chips, rows, mine)
    at = lambda d: lax.broadcasted_iota(jnp.int32, shape, d)
    which = at(2) * blocks + (2 * at(1) + (at(0) ^ core)) * mine + at(3)
    which = which.reshape(-1)
    member = ((starts[:, None] <= which[None, :]) & (which[None, :] < ends[:, None])).astype(b16)
    stacked = jnp.stack([near, far]).reshape(-1, units, width)
    summed = jnp.einsum("db,buc->udc", member, stacked, preferred_element_type=f32)
    docgrad = (summed / block_counts.astype(f32)[None, :, None]).astype(b16)

    ratio = rows // feats
    far_off = jnp.int32(1 << 20)
    start = jnp.where(row // ratio == feat, row % ratio * units, far_off)
    diag = inverse_diag.reshape(units, width)
    chunks = rows // 2
    side = row % 2
    sent = dense_half(1 - side, start, docgrad, diag, inverse_dense, b16)
    kept = dense_half(side, start, docgrad, diag, inverse_dense, f32)
    half = kept + swap(sent, "rows", 1).astype(f32)
    half = half.reshape(chunks, docs // chunks, -1)
    place = row // 2
    own = pick(half, place)
    for k in range(1, chunks):
        own = own + swap(pick(half, place ^ k).astype(b16), "rows", 2 * k).astype(f32)
    own = own.astype(b16)
    own = jnp.stack([own] + [swap(own, "rows", 2 * k) for k in range(1, chunks)])
    other = swap(own, "rows", 1)
    scores = score(side, place, own, other, train_grads)

    scores = scores.reshape(feats, docs // feats, -1)
    mask = 1
    while mask < feats:
        left = scores.reshape(scores.shape[0] // 2, 2, docs // feats, -1)
        bit = (feat // mask) % 2
        scores = pick(left, bit, 1) + swap(pick(left, 1 - bit, 1), "feat", mask)
        mask *= 2
    return scores[0]


def solution(mesh):
    in_specs = (
        P("rows", "feat"),
        P("rows", "feat"),
        P("feat", None),
        P("feat", None),
        P("rows"),
        P(),
        P("rows", "feat"),
        P("rows"),
        P("rows", "feat"),
    )
    out_specs = P("feat", "rows")
    return jax.shard_map(
        per_device, mesh=mesh, in_specs=in_specs, out_specs=out_specs, check_vma=False
    )
```

```python
import jax
import jax.numpy as jnp
from jax import lax
from jax.experimental import pallas as pl
from jax.experimental.pallas import tpu as pltpu
from jax.sharding import PartitionSpec as P

BLOCK = 128
LANES = 128


def swap(x, axis, mask):
    count = lax.axis_size(axis)
    return lax.ppermute(x, axis, [(i, i ^ mask) for i in range(count)])


def pick(x, index, axis=0):
    return lax.dynamic_index_in_dim(x, index, axis, keepdims=False)


def in_hbm(x):
    return pltpu.with_memory_space_constraint(x, pltpu.HBM)


def project_kernel(core_ref, acts_ref, grads_ref, in_ref, out_ref, kept_ref, sent_ref, sum_ref):
    step = pl.program_id(0)
    tokens = acts_ref.shape[0]
    pairs, part = kept_ref.shape[1], kept_ref.shape[2]
    for i, (left_ref, right_ref) in enumerate(((acts_ref, in_ref), (grads_ref, out_ref))):
        piece = jnp.dot(left_ref[...], right_ref[...], preferred_element_type=jnp.float32)

        @pl.when(step == 0)
        def _():
            sum_ref[i] = piece

        @pl.when(step > 0)
        def _():
            sum_ref[i] += piece

    @pl.when(step == pl.num_programs(0) - 1)
    def _():
        core = core_ref[0]
        for i in range(2):
            for p in range(pairs):
                base = 2 * p * part
                kept_ref[i, p] = sum_ref[i, pl.ds(base + core * part, part), :]
                sent_ref[i, p] = sum_ref[i, pl.ds(base + (1 - core) * part, part), :]


def project(core, acts, grads, proj_in, proj_out, feats):
    tokens, depth = acts.shape
    width = proj_in.shape[1]
    tile = min(512, depth)
    shape = (2, feats // 2, tokens // feats, width)
    whole = pl.BlockSpec(shape, lambda k, s: (0, 0, 0, 0))
    return pl.pallas_call(
        project_kernel,
        out_shape=[jax.ShapeDtypeStruct(shape, jnp.float32)] * 2,
        grid_spec=pltpu.PrefetchScalarGridSpec(
            num_scalar_prefetch=1,
            grid=(depth // tile,),
            in_specs=[
                pl.BlockSpec((tokens, tile), lambda k, s: (0, k)),
                pl.BlockSpec((tokens, tile), lambda k, s: (0, k)),
                pl.BlockSpec((tile, width), lambda k, s: (k, 0)),
                pl.BlockSpec((tile, width), lambda k, s: (k, 0)),
            ],
            out_specs=[whole, whole],
            scratch_shapes=[pltpu.VMEM((2, tokens, width), jnp.float32)],
        ),
        compiler_params=pltpu.CompilerParams(vmem_limit_bytes=24 << 20),
    )(core.reshape(1).astype(jnp.int32), in_hbm(acts), in_hbm(grads), in_hbm(proj_in), in_hbm(proj_out))


def dense_kernel(half_ref, grad_ref, diag_ref, inverse_ref, out_ref):
    units, docs, _ = grad_ref.shape
    left = jnp.concatenate([grad_ref[a] for a in range(units)], axis=1)
    total = jnp.dot(left, inverse_ref[...], preferred_element_type=jnp.float32)
    out_ref[0] = total.astype(out_ref.dtype)
    wide = out_ref.shape[2] // LANES
    first = (half_ref[0] * pl.num_programs(0) + pl.program_id(0)) * wide - half_ref[1]
    for q in range(wide):
        unit = first + q

        @pl.when((unit >= 0) & (unit < units))
        def _():
            at = jnp.clip(unit, 0, units - 1)
            term = grad_ref[at].astype(jnp.float32) * diag_ref[pl.ds(at, 1), :]
            cols = slice(q * LANES, (q + 1) * LANES)
            out_ref[0, :, cols] = (total[:, cols] + term).astype(out_ref.dtype)


def dense_half(half, start, docgrad, diag, inverse, dtype):
    units, docs, _ = docgrad.shape
    depth, cols = inverse.shape
    quarter = cols // 4
    wide = min(512, quarter)
    each = quarter // wide
    return pl.pallas_call(
        dense_kernel,
        out_shape=jax.ShapeDtypeStruct((2, docs, quarter), dtype),
        grid_spec=pltpu.PrefetchScalarGridSpec(
            num_scalar_prefetch=1,
            grid=(2 * each,),
            in_specs=[
                pl.BlockSpec((units, docs, LANES), lambda n, s: (0, 0, 0)),
                pl.BlockSpec((units, LANES), lambda n, s: (0, 0)),
                pl.BlockSpec((depth, wide), lambda n, s: (0, s[0] * 2 * each + n)),
            ],
            out_specs=pl.BlockSpec((1, docs, wide), lambda n, s: (n // each, 0, n % each)),
        ),
        compiler_params=pltpu.CompilerParams(vmem_limit_bytes=24 << 20),
    )(jnp.stack([half, start]).astype(jnp.int32), docgrad, diag, in_hbm(inverse))


def score_kernel(where_ref, near_ref, far_ref, *refs):
    out_ref = refs[-1]
    train_ref = refs[-2]
    step = pl.program_id(0)

    def part(ref):
        return lax.dot_general(
            ref[...], train_ref[...], (((1,), (1,)), ((), ())), preferred_element_type=jnp.float32
        )

    @pl.when(step == 0)
    def _():
        got = part(near_ref)
        out_ref[...] = got + refs[0][...] if len(refs) == 3 else got

    @pl.when(step == 1)
    def _():
        out_ref[...] += part(far_ref)


def score(side, turn, near, far, before, train):
    docs, quarter = near.shape
    count = train.shape[0]
    full = lambda *shape: pl.BlockSpec(shape, lambda n, s: (0,) * len(shape))
    return pl.pallas_call(
        score_kernel,
        out_shape=jax.ShapeDtypeStruct((docs, count), jnp.float32),
        grid_spec=pltpu.PrefetchScalarGridSpec(
            num_scalar_prefetch=1,
            grid=(2,),
            in_specs=[full(docs, quarter), full(docs, quarter)]
            + [full(docs, count)] * len(before)
            + [pl.BlockSpec((count, quarter), lambda n, s: (0, 2 * s[0] + (s[1] ^ n)))],
            out_specs=full(docs, count),
        ),
        compiler_params=pltpu.CompilerParams(vmem_limit_bytes=24 << 20),
    )(jnp.stack([side, turn]).astype(jnp.int32), near, far, *before, in_hbm(train))


def per_device(
    acts,
    grads_out,
    proj_in,
    proj_out,
    doc_ids,
    block_counts,
    inverse_dense,
    inverse_diag,
    train_grads,
):
    tokens = acts.shape[0]
    rows = lax.axis_size("rows")
    feats = lax.axis_size("feat")
    row = lax.axis_index("rows")
    feat = lax.axis_index("feat")
    width = proj_in.shape[1]
    docs = block_counts.shape[0]
    part = tokens // feats
    mine = part // BLOCK
    f32, b16 = jnp.float32, jnp.bfloat16

    both, sent = project(feat % 2, acts, grads_out, proj_in, proj_out, feats)
    both = both + swap(sent, "feat", 1)
    mask = 2
    while mask < feats:
        left = both.reshape(2, both.shape[1] // 2, 2, part, width)
        bit = (feat // mask) % 2
        sent = pick(left, 1 - bit, 2).astype(b16)
        both = pick(left, bit, 2) + swap(sent, "feat", mask).astype(f32)
        mask *= 2
    xin = both[0].reshape(mine, BLOCK, width).astype(b16)
    gout = both[1].reshape(mine, BLOCK, width).astype(b16)

    order = jnp.arange(docs, dtype=jnp.int32)
    starts = jnp.sum(jnp.where(order[None, :] < order[:, None], block_counts[None, :], 0), axis=1)
    ends = starts + block_counts
    blocks = tokens // BLOCK
    here = row * blocks + feat * mine + jnp.arange(mine, dtype=jnp.int32)
    owner = jnp.sum((starts[None, :] <= here[:, None]).astype(jnp.int32), axis=1) - 1
    ids = pick(doc_ids.reshape(feats, mine, BLOCK), feat)
    gmask = jnp.where((ids == owner[:, None])[:, :, None], gout, jnp.zeros_like(gout))
    sums = jnp.einsum("kta,ktc->kac", gmask, xin, preferred_element_type=f32).astype(b16)

    units = width // rows
    chips = feats // 2
    parts = sums.reshape(mine, rows, units, width).transpose(1, 0, 2, 3)
    parts = jnp.broadcast_to(parts[None], (chips,) + parts.shape).reshape(chips * rows, mine, units, width)
    groups = [[(2 * x + c) * rows + r for x in range(chips) for r in range(rows)] for c in range(2)]
    near = lax.all_to_all(parts, ("feat", "rows"), 0, 0, tiled=True, axis_index_groups=groups)
    far = swap(near, "feat", 1)
    core = feat % 2
    shape = (2, chips, rows, mine)
    at = lambda d: lax.broadcasted_iota(jnp.int32, shape, d)
    which = at(2) * blocks + (2 * at(1) + (at(0) ^ core)) * mine + at(3)
    which = which.reshape(-1)
    member = ((starts[:, None] <= which[None, :]) & (which[None, :] < ends[:, None])).astype(b16)
    stacked = jnp.stack([near, far]).reshape(-1, units, width)
    summed = jnp.einsum("db,buc->udc", member, stacked, preferred_element_type=f32)
    docgrad = (summed / block_counts.astype(f32)[None, :, None]).astype(b16)

    ratio = rows // feats
    far_off = jnp.int32(1 << 20)
    start = jnp.where(row // ratio == feat, row % ratio * units, far_off)
    diag = inverse_diag.reshape(units, width)
    side = row % 2
    turn = row // 2 % 2
    sent = dense_half(1 - side, start, docgrad, diag, inverse_dense, b16)
    kept = dense_half(side, start, docgrad, diag, inverse_dense, f32)
    half = kept + swap(sent, "rows", 1).astype(f32)
    own = pick(half, turn) + swap(pick(half, 1 - turn).astype(b16), "rows", 2).astype(f32)
    mask = 4
    while mask < rows:
        own = own + swap(own.astype(b16), "rows", mask).astype(f32)
        mask *= 2
    own = own.astype(b16)
    next_ = swap(own, "rows", 2)
    own_y = swap(own, "rows", 1)
    next_y = swap(next_, "rows", 1)
    scores = score(side, turn, own, next_, (), train_grads)
    scores = score(1 - side, turn, own_y, next_y, (scores,), train_grads)

    scores = scores.reshape(feats, docs // feats, -1)
    mask = 1
    while mask < feats:
        left = scores.reshape(scores.shape[0] // 2, 2, docs // feats, -1)
        bit = (feat // mask) % 2
        scores = pick(left, bit, 1) + swap(pick(left, 1 - bit, 1), "feat", mask)
        mask *= 2
    return scores[0]


def solution(mesh):
    in_specs = (
        P("rows", "feat"),
        P("rows", "feat"),
        P("feat", None),
        P("feat", None),
        P("rows"),
        P(),
        P("rows", "feat"),
        P("rows"),
        P("rows", "feat"),
    )
    out_specs = P("feat", "rows")
    return jax.shard_map(
        per_device, mesh=mesh, in_specs=in_specs, out_specs=out_specs, check_vma=False
    )
```

```python
import jax
import jax.numpy as jnp
from jax import lax
from jax.experimental import pallas as pl
from jax.experimental.pallas import tpu as pltpu
from jax.sharding import PartitionSpec as P

BLOCK = 128
LANES = 128


def swap(x, axis, mask):
    count = lax.axis_size(axis)
    return lax.ppermute(x, axis, [(i, i ^ mask) for i in range(count)])


def pick(x, index, axis=0):
    return lax.dynamic_index_in_dim(x, index, axis, keepdims=False)


def in_hbm(x):
    return pltpu.with_memory_space_constraint(x, pltpu.HBM)


def in_vmem(x):
    return pltpu.with_memory_space_constraint(x, pltpu.VMEM)


def turn_kernel(source_ref, out_ref):
    out_ref[...] = source_ref[...].T


def turned(x):
    count, cols = x.shape
    wide = min(512, cols)
    return pl.pallas_call(
        turn_kernel,
        out_shape=jax.ShapeDtypeStruct((cols, count), x.dtype),
        grid=(cols // wide,),
        in_specs=[pl.BlockSpec((count, wide), lambda n: (0, n))],
        out_specs=pl.BlockSpec((wide, count), lambda n: (n, 0)),
        compiler_params=pltpu.CompilerParams(vmem_limit_bytes=20 << 20),
    )(in_hbm(x))


def dense_kernel(half_ref, grad_ref, diag_ref, source_ref, out_ref, inverse_ref, sems):
    units, _, _ = grad_ref.shape
    pieces, _, wide = out_ref.shape
    half = pieces * wide
    steps = sems.shape[0]
    tile = half // steps
    copies = []
    for n in range(steps):
        at = pl.multiple_of(half_ref[0] * half + n * tile, tile)
        place = inverse_ref.at[:, pl.ds(n * tile, tile)]
        copies.append(pltpu.make_async_copy(source_ref.at[:, pl.ds(at, tile)], place, sems.at[n]))
    for copy in copies:
        copy.start()
    left = jnp.concatenate([grad_ref[a] for a in range(units)], axis=1)
    for n in range(steps):
        copies[n].wait()
        total = jnp.dot(
            left, inverse_ref[:, n * tile : (n + 1) * tile], preferred_element_type=jnp.float32
        )
        piece, col = n * tile // wide, n * tile % wide
        out_ref[piece, :, col : col + tile] = total.astype(out_ref.dtype)
        for q in range(tile // LANES):
            unit = (half_ref[0] * half + n * tile) // LANES + q - half_ref[1]

            @pl.when((unit >= 0) & (unit < units))
            def _():
                a = jnp.clip(unit, 0, units - 1)
                term = grad_ref[a].astype(jnp.float32) * diag_ref[pl.ds(a, 1), :]
                part = total[:, q * LANES : (q + 1) * LANES] + term
                cols = slice(col + q * LANES, col + (q + 1) * LANES)
                out_ref[piece, :, cols] = part.astype(out_ref.dtype)


SMEM = pl.BlockSpec(memory_space=pltpu.SMEM)
VMEM = pl.BlockSpec(memory_space=pltpu.VMEM)


def dense_half(half, start, docgrad, diag, inverse, dtype):
    _, docs, _ = docgrad.shape
    depth, cols = inverse.shape
    return pl.pallas_call(
        dense_kernel,
        out_shape=jax.ShapeDtypeStruct((2, docs, cols // 4), dtype),
        in_specs=[SMEM, VMEM, VMEM, pl.BlockSpec(memory_space=pltpu.HBM)],
        out_specs=VMEM,
        scratch_shapes=[
            pltpu.VMEM((depth, cols // 2), inverse.dtype),
            pltpu.SemaphoreType.DMA((cols // 2 // min(512, cols // 4),)),
        ],
        compiler_params=pltpu.CompilerParams(vmem_limit_bytes=20 << 20),
    )(jnp.stack([half, start]).astype(jnp.int32), docgrad, diag, in_hbm(inverse))


def score_kernel(where_ref, near_ref, far_ref, *refs):
    out_ref = refs[-1]
    train_ref = refs[-2]
    quarter = near_ref.shape[1]
    total = refs[0][...] if len(refs) == 3 else None
    for i, ref in enumerate((near_ref, far_ref)):
        at = pl.multiple_of((2 * where_ref[0] + (where_ref[1] ^ i)) * quarter, quarter)
        got = jnp.dot(ref[...], train_ref[pl.ds(at, quarter), :], preferred_element_type=jnp.float32)
        total = got if total is None else total + got
    out_ref[...] = total


def score(side, turn, near, far, before, train):
    docs, _ = near.shape
    count = train.shape[1]
    return pl.pallas_call(
        score_kernel,
        out_shape=jax.ShapeDtypeStruct((docs, count), jnp.float32),
        in_specs=[SMEM, VMEM, VMEM] + [VMEM] * len(before) + [VMEM],
        out_specs=VMEM,
        compiler_params=pltpu.CompilerParams(vmem_limit_bytes=20 << 20),
    )(jnp.stack([side, turn]).astype(jnp.int32), near, far, *before, in_vmem(train))


def per_device(
    acts,
    grads_out,
    proj_in,
    proj_out,
    doc_ids,
    block_counts,
    inverse_dense,
    inverse_diag,
    train_grads,
):
    tokens = acts.shape[0]
    rows = lax.axis_size("rows")
    feats = lax.axis_size("feat")
    row = lax.axis_index("rows")
    feat = lax.axis_index("feat")
    width = proj_in.shape[1]
    docs = block_counts.shape[0]
    part = tokens // feats
    mine = part // BLOCK
    f32, b16 = jnp.float32, jnp.bfloat16

    def across(left, right):
        both = jnp.dot(left, right, preferred_element_type=f32).reshape(feats, part, width)
        mask = 1
        while mask < feats:
            pairs = both.reshape(both.shape[0] // 2, 2, part, width)
            bit = (feat // mask) % 2
            sent = pick(pairs, 1 - bit, 1).astype(f32 if mask == 1 else b16)
            both = pick(pairs, bit, 1) + swap(sent, "feat", mask).astype(f32)
            mask *= 2
        return both.reshape(mine, BLOCK, width).astype(b16)

    xin = across(acts, proj_in)
    gout = across(grads_out, proj_out)

    order = jnp.arange(docs, dtype=jnp.int32)
    starts = jnp.sum(jnp.where(order[None, :] < order[:, None], block_counts[None, :], 0), axis=1)
    ends = starts + block_counts
    blocks = tokens // BLOCK
    here = row * blocks + feat * mine + jnp.arange(mine, dtype=jnp.int32)
    owner = jnp.sum((starts[None, :] <= here[:, None]).astype(jnp.int32), axis=1) - 1
    ids = pick(doc_ids.reshape(feats, mine, BLOCK), feat)
    gmask = jnp.where((ids == owner[:, None])[:, :, None], gout, jnp.zeros_like(gout))
    sums = jnp.einsum("kta,ktc->kac", gmask, xin, preferred_element_type=f32).astype(b16)

    units = width // rows
    chips = feats // 2
    parts = sums.reshape(mine, rows, units, width).transpose(1, 0, 2, 3)
    parts = jnp.broadcast_to(parts[None], (chips,) + parts.shape).reshape(chips * rows, mine, units, width)
    groups = [[(2 * x + c) * rows + r for x in range(chips) for r in range(rows)] for c in range(2)]
    near = lax.all_to_all(parts, ("feat", "rows"), 0, 0, tiled=True, axis_index_groups=groups)
    train = turned(train_grads)
    far = swap(near, "feat", 1)
    core = feat % 2
    shape = (chips, rows, mine)
    at = lambda d: lax.broadcasted_iota(jnp.int32, shape, d)

    def gathered(sums, side):
        which = (at(1) * blocks + (2 * at(0) + side) * mine + at(2)).reshape(-1)
        member = (starts[:, None] <= which[None, :]) & (which[None, :] < ends[:, None])
        sums = sums.reshape(-1, units, width)
        return jnp.einsum("db,buc->udc", member.astype(b16), sums, preferred_element_type=f32)

    summed = gathered(near, core) + gathered(far, 1 - core)
    docgrad = (summed / block_counts.astype(f32)[None, :, None]).astype(b16)

    ratio = rows // feats
    far_off = jnp.int32(1 << 20)
    start = jnp.where(row // ratio == feat, row % ratio * units, far_off)
    diag = inverse_diag.reshape(units, width)
    side = row % 2
    turn = row // 2 % 2
    sent = dense_half(1 - side, start, docgrad, diag, inverse_dense, b16)
    kept = dense_half(side, start, docgrad, diag, inverse_dense, f32)
    half = kept + swap(sent, "rows", 1).astype(f32)
    own = pick(half, turn) + swap(pick(half, 1 - turn).astype(b16), "rows", 2).astype(f32)
    mask = 4
    while mask < rows:
        own = own + swap(own.astype(b16), "rows", mask).astype(f32)
        mask *= 2
    own = own.astype(b16)
    next_ = swap(own, "rows", 2)
    own_y = swap(own, "rows", 1)
    next_y = swap(next_, "rows", 1)
    scores = score(side, turn, own, next_, (), train)
    scores = score(1 - side, turn, own_y, next_y, (scores,), train)

    scores = scores.reshape(feats, docs // feats, -1)
    mask = 1
    while mask < feats:
        left = scores.reshape(scores.shape[0] // 2, 2, docs // feats, -1)
        bit = (feat // mask) % 2
        scores = pick(left, bit, 1) + swap(pick(left, 1 - bit, 1), "feat", mask)
        mask *= 2
    return scores[0]


def solution(mesh):
    in_specs = (
        P("rows", "feat"),
        P("rows", "feat"),
        P("feat", None),
        P("feat", None),
        P("rows"),
        P(),
        P("rows", "feat"),
        P("rows"),
        P("rows", "feat"),
    )
    out_specs = P("feat", "rows")
    return jax.shard_map(
        per_device, mesh=mesh, in_specs=in_specs, out_specs=out_specs, check_vma=False
    )
```

```python
import jax
import jax.numpy as jnp
from jax import lax
from jax.experimental import pallas as pl
from jax.experimental.pallas import tpu as pltpu
from jax.sharding import PartitionSpec as P


BLOCK = 128
LANES = 128
SMEM = pl.BlockSpec(memory_space=pltpu.SMEM)
VMEM = pl.BlockSpec(memory_space=pltpu.VMEM)
HBM = pl.BlockSpec(memory_space=pltpu.HBM)
CORE, FEAT, SIDE, TURN, PLACE, START = range(6)


def swap(x, axis, mask):
    count = lax.axis_size(axis)
    return lax.ppermute(x, axis, [(i, i ^ mask) for i in range(count)])


def pick(x, index, axis=0):
    return lax.dynamic_index_in_dim(x, index, axis, keepdims=False)


def in_hbm(x):
    return pltpu.with_memory_space_constraint(x, pltpu.HBM)


def limit(mib):
    return pltpu.CompilerParams(vmem_limit_bytes=mib << 20)


def sums_kernel(blocks, rows_ref, where_ref, counts_ref, ids_ref, kx_ref, rx_ref, kg_ref, rg_ref, *refs):
    outs, sums_ref = refs[:-1], refs[-1]
    mine = sums_ref.shape[0]
    docs = counts_ref.shape[0]
    xin = (kx_ref[...] + rx_ref[...].astype(jnp.float32)).astype(jnp.bfloat16)
    gout = (kg_ref[...] + rg_ref[...].astype(jnp.float32)).astype(jnp.bfloat16)
    for j in range(mine):
        local = where_ref[FEAT] * mine + j
        block = rows_ref[0] * blocks + local

        def count(d, carry):
            first, owner = carry
            return first + counts_ref[d], owner + (first <= block).astype(jnp.int32)

        _, owner = lax.fori_loop(0, docs, count, (jnp.int32(0), jnp.int32(-1)), unroll=True)
        keep = ids_ref[pl.ds(local, 1), :] == owner
        part = slice(j * BLOCK, (j + 1) * BLOCK)
        turned = gout[part].astype(jnp.float32).T
        masked = jnp.where(keep, turned, 0.0).astype(jnp.bfloat16)
        sums_ref[j] = jnp.dot(masked, xin[part], preferred_element_type=jnp.float32)
    few = outs[0].shape[0] // mine
    for k, out_ref in enumerate(outs):
        at = pl.multiple_of((where_ref[PLACE] ^ k) * few, few)
        for j in range(mine):
            piece = sums_ref[j, pl.ds(at, few), :]
            out_ref[j * few : (j + 1) * few] = piece.astype(out_ref.dtype)


def block_sums(row, where, counts, ids, kept_x, recv_x, kept_g, recv_g, blocks, places):
    part, width = kept_x.shape
    mine = part // BLOCK
    few = width // places
    shape = jax.ShapeDtypeStruct((mine * few, width), jnp.bfloat16)

    def kernel(*refs):
        sums_kernel(blocks, *refs)

    return pl.pallas_call(
        kernel,
        out_shape=[shape] * places,
        in_specs=[SMEM, SMEM, SMEM] + [VMEM] * 5,
        out_specs=[VMEM] * places,
        scratch_shapes=[pltpu.VMEM((mine, width, width), jnp.float32)],
        compiler_params=limit(8),
        name="sums",
    )(row, where, counts, ids, kept_x, recv_x, kept_g, recv_g)


def deal(where, arrays, mine):
    rows, width = arrays[0].shape
    shape = jax.ShapeDtypeStruct((len(arrays) * rows // 2, width), arrays[0].dtype)

    def kernel(where_ref, *refs):
        own_ref, other_ref = refs[-2:]
        first = where_ref[SIDE] == 0
        few = rows // mine
        half = few // 2
        for k, ref in enumerate(refs[:-2]):
            got = ref[...].astype(jnp.float32)
            for j in range(mine):
                low, high = got[j * few : j * few + half], got[j * few + half : (j + 1) * few]
                at = slice((k * mine + j) * half, (k * mine + j + 1) * half)
                own_ref[at] = jnp.where(first, low, high).astype(own_ref.dtype)
                other_ref[at] = jnp.where(first, high, low).astype(own_ref.dtype)

    return pl.pallas_call(
        kernel,
        out_shape=[shape, shape],
        in_specs=[SMEM] + [VMEM] * len(arrays),
        out_specs=[VMEM, VMEM],
        compiler_params=limit(4),
        name="deal",
    )(where, *arrays)


def members(where, counts, units, mine, places, pairs, blocks):
    docs = counts.shape[0]
    cols = units * mine * places * pairs * 4

    def kernel(where_ref, counts_ref, member_ref, broad_ref):
        doc = lax.broadcasted_iota(jnp.int32, (docs, LANES), 0)
        starts = jnp.zeros((docs, LANES), jnp.int32)
        broad = jnp.zeros((docs, LANES), jnp.int32)
        for d in range(docs):
            starts += jnp.where(doc > d, counts_ref[d], 0)
            broad += jnp.where(doc == d, counts_ref[d], 0)
        broad_ref[...] = broad.astype(jnp.float32)
        ends = starts + broad
        side, place, feat = where_ref[SIDE], where_ref[PLACE], where_ref[FEAT]
        for n in range(cols // LANES):
            col = lax.broadcasted_iota(jnp.int32, (docs, LANES), 1) + n * LANES
            at, cut = [], col
            for size in (units, mine, places, pairs, 2, 2):
                bits = size.bit_length() - 1
                at.append(cut & (size - 1))
                cut = lax.shift_right_logical(cut, bits)
            unit, j, k, x, y, c = at
            from_row = 2 * (place ^ k) + (side ^ y)
            which = from_row * blocks + (feat ^ (2 * x) ^ c) * mine + j
            holds = (starts <= which) & (which < ends)
            for u in range(units):
                part = jnp.where(holds & (unit == u), 1.0, 0.0).astype(jnp.bfloat16)
                member_ref[u * docs : (u + 1) * docs, n * LANES : (n + 1) * LANES] = part

    return pl.pallas_call(
        kernel,
        out_shape=[
            jax.ShapeDtypeStruct((units * docs, cols), jnp.bfloat16),
            jax.ShapeDtypeStruct((docs, LANES), jnp.float32),
        ],
        in_specs=[SMEM, SMEM],
        out_specs=[VMEM, VMEM],
        compiler_params=limit(4),
        name="members",
    )(where, counts)


def begin(source_ref, base, held_ref, sems):
    tile = held_ref.shape[1] // sems.shape[0]
    copies = []
    for n in range(sems.shape[0]):
        at = pl.multiple_of(base + n * tile, tile)
        place = held_ref.at[:, pl.ds(n * tile, tile)]
        copies.append(pltpu.make_async_copy(source_ref.at[:, pl.ds(at, tile)], place, sems.at[n]))
    for copy in copies:
        copy.start()
    return copies


def fetch(where, inverse, other):
    depth, cols = inverse.shape
    quarter = cols // 4

    def kernel(where_ref, source_ref, out_ref, sems):
        half = 1 - where_ref[SIDE] if other else where_ref[SIDE]
        for copy in begin(source_ref, half * 2 * quarter, out_ref, sems):
            copy.wait()

    return pl.pallas_call(
        kernel,
        out_shape=jax.ShapeDtypeStruct((depth, quarter), inverse.dtype),
        in_specs=[SMEM, HBM],
        out_specs=VMEM,
        scratch_shapes=[pltpu.SemaphoreType.DMA((tiles(quarter),))],
        compiler_params=limit(6),
        name="fetch",
    )(where, in_hbm(inverse))


def tiles(quarter):
    return max(quarter // 512, 1)


def dense_body(where_ref, make_left, grad_ref, diag_ref, ready_ref, source_ref, out_ref, held_ref, sems, half):
    units = grad_ref.shape[0]
    quarter = out_ref.shape[2]
    steps = sems.shape[0]
    tile = quarter // steps
    copies = begin(source_ref, (2 * half + 1) * quarter, held_ref, sems)
    left = make_left()
    for piece in range(2):
        for n in range(steps):
            col = n * tile
            if piece:
                copies[n].wait()
            ref = held_ref if piece else ready_ref
            total = jnp.dot(left, ref[:, col : col + tile], preferred_element_type=jnp.float32)
            out_ref[piece, :, col : col + tile] = total.astype(out_ref.dtype)
            base = (2 * half + piece) * quarter + col
            for q in range(tile // LANES):
                unit = base // LANES + q - where_ref[START]

                @pl.when((unit >= 0) & (unit < units))
                def _():
                    a = jnp.clip(unit, 0, units - 1)
                    term = grad_ref[a].astype(jnp.float32) * diag_ref[pl.ds(a, 1), :]
                    part = total[:, q * LANES : (q + 1) * LANES] + term
                    cols = slice(col + q * LANES, col + (q + 1) * LANES)
                    out_ref[piece, :, cols] = part.astype(out_ref.dtype)


def joined(grad_ref):
    return jnp.concatenate([grad_ref[u] for u in range(grad_ref.shape[0])], axis=1)


def first_kernel(where_ref, member_ref, counts_ref, diag_ref, ready_ref, source_ref, *refs):
    arrays, (out_ref, grad_ref, held_ref, sems) = refs[:-4], refs[-4:]
    units, docs, _ = grad_ref.shape
    each = arrays[0].shape[0]

    def make_left():
        summed = None
        for s, ref in enumerate(arrays):
            part = jnp.dot(
                member_ref[:, s * each : (s + 1) * each],
                ref[...],
                preferred_element_type=jnp.float32,
            )
            summed = part if summed is None else summed + part
        for u in range(units):
            mean = summed[u * docs : (u + 1) * docs] / counts_ref[...]
            grad_ref[u] = mean.astype(grad_ref.dtype)
        return joined(grad_ref)

    half = 1 - where_ref[SIDE]
    dense_body(
        where_ref, make_left, grad_ref, diag_ref, ready_ref, source_ref, out_ref, held_ref, sems, half
    )


def held_scratch(inverse):
    quarter = inverse.shape[1] // 4
    return [
        pltpu.VMEM((inverse.shape[0], quarter), inverse.dtype),
        pltpu.SemaphoreType.DMA((tiles(quarter),)),
    ]


def dense_first(where, member, counts, diag, ready, inverse, arrays, units):
    docs = counts.shape[0]
    return pl.pallas_call(
        first_kernel,
        out_shape=[
            jax.ShapeDtypeStruct((2, docs, inverse.shape[1] // 4), jnp.bfloat16),
            jax.ShapeDtypeStruct((units, docs, LANES), jnp.bfloat16),
        ],
        in_specs=[SMEM] + [VMEM] * 4 + [HBM] + [VMEM] * len(arrays),
        out_specs=[VMEM, VMEM],
        scratch_shapes=held_scratch(inverse),
        compiler_params=limit(16),
        name="first",
    )(where, member, counts, diag, ready, in_hbm(inverse), *arrays)


def second_kernel(where_ref, grad_ref, diag_ref, ready_ref, source_ref, out_ref, held_ref, sems):
    make_left = lambda: joined(grad_ref)
    half = where_ref[SIDE]
    dense_body(
        where_ref, make_left, grad_ref, diag_ref, ready_ref, source_ref, out_ref, held_ref, sems, half
    )


def dense_second(where, docgrad, diag, ready, inverse):
    docs = docgrad.shape[1]
    return pl.pallas_call(
        second_kernel,
        out_shape=jax.ShapeDtypeStruct((2, docs, inverse.shape[1] // 4), jnp.float32),
        in_specs=[SMEM] + [VMEM] * 3 + [HBM],
        out_specs=VMEM,
        scratch_shapes=held_scratch(inverse),
        compiler_params=limit(16),
        name="second",
    )(where, docgrad, diag, ready, in_hbm(inverse))


def split_kernel(where_ref, kept_ref, recv_ref, own_ref, sent_ref):
    turn = where_ref[TURN]
    own_ref[...] = kept_ref[turn] + recv_ref[turn].astype(jnp.float32)
    sent = kept_ref[1 - turn] + recv_ref[1 - turn].astype(jnp.float32)
    sent_ref[...] = sent.astype(sent_ref.dtype)


def split(where, kept, recv):
    shape = kept.shape[1:]
    return pl.pallas_call(
        split_kernel,
        out_shape=[
            jax.ShapeDtypeStruct(shape, jnp.float32),
            jax.ShapeDtypeStruct(shape, jnp.bfloat16),
        ],
        in_specs=[SMEM, VMEM, VMEM],
        out_specs=[VMEM, VMEM],
        compiler_params=limit(4),
        name="split",
    )(where, kept, recv)


def turned(where, train, other):
    count, cols = train.shape
    half = cols // 2
    steps = 4
    tile = half // steps

    def kernel(where_ref, source_ref, out_ref, held_ref, sems):
        which = 1 - where_ref[SIDE] if other else where_ref[SIDE]
        copies = []
        for n in range(steps):
            at = pl.multiple_of(which * half + n * tile, tile)
            place = held_ref.at[:, pl.ds(n * tile, tile)]
            copies.append(pltpu.make_async_copy(source_ref.at[:, pl.ds(at, tile)], place, sems.at[n]))
        for copy in copies:
            copy.start()
        for n in range(steps):
            copies[n].wait()
            part = slice(n * tile, (n + 1) * tile)
            out_ref[part, :] = held_ref[:, part].T

    return pl.pallas_call(
        kernel,
        out_shape=jax.ShapeDtypeStruct((half, count), train.dtype),
        in_specs=[SMEM, HBM],
        out_specs=VMEM,
        scratch_shapes=[
            pltpu.VMEM((count, half), train.dtype),
            pltpu.SemaphoreType.DMA((steps,)),
        ],
        compiler_params=limit(8),
        name="turned",
    )(where, in_hbm(train))


def score_part(where_ref, near_ref, far_ref, train_ref):
    quarter = near_ref.shape[1]
    total = None
    for i, ref in enumerate((near_ref, far_ref)):
        at = pl.multiple_of((where_ref[TURN] ^ i) * quarter, quarter)
        got = jnp.dot(ref[...], train_ref[pl.ds(at, quarter), :], preferred_element_type=jnp.float32)
        total = got if total is None else total + got
    return total


def score_near(where, near, far, train):
    def kernel(where_ref, near_ref, far_ref, train_ref, out_ref):
        out_ref[...] = score_part(where_ref, near_ref, far_ref, train_ref)

    return pl.pallas_call(
        kernel,
        out_shape=jax.ShapeDtypeStruct((near.shape[0], train.shape[1]), jnp.float32),
        in_specs=[SMEM] + [VMEM] * 3,
        out_specs=VMEM,
        compiler_params=limit(4),
        name="near",
    )(where, near, far, train)


def score_far(where, near, far, before, train, feats):
    docs, count = before.shape
    few = docs // feats
    shape = jax.ShapeDtypeStruct((feats // 2, few, count), jnp.float32)

    def kernel(where_ref, near_ref, far_ref, before_ref, train_ref, kept_ref, sent_ref, all_ref):
        all_ref[...] = before_ref[...] + score_part(where_ref, near_ref, far_ref, train_ref)
        for p in range(feats // 2):
            for ref, core in ((kept_ref, where_ref[CORE]), (sent_ref, 1 - where_ref[CORE])):
                at = pl.multiple_of((2 * p + core) * few, few)
                ref[p] = all_ref[pl.ds(at, few), :]

    return pl.pallas_call(
        kernel,
        out_shape=[shape, shape],
        in_specs=[SMEM] + [VMEM] * 4,
        out_specs=[VMEM, VMEM],
        scratch_shapes=[pltpu.VMEM((docs, count), jnp.float32)],
        compiler_params=limit(4),
        name="far",
    )(where, near, far, before, train)


def per_device(
    acts,
    grads_out,
    proj_in,
    proj_out,
    doc_ids,
    block_counts,
    inverse_dense,
    inverse_diag,
    train_grads,
):
    tokens = acts.shape[0]
    rows = lax.axis_size("rows")
    feats = lax.axis_size("feat")
    row = lax.axis_index("rows")
    feat = lax.axis_index("feat")
    width = proj_in.shape[1]
    docs = block_counts.shape[0]
    part = tokens // feats
    mine = part // BLOCK
    blocks = tokens // BLOCK
    units = width // rows
    places = rows // 2
    ratio = rows // feats
    f32, b16 = jnp.float32, jnp.bfloat16

    core, side, turn, place = feat & 1, row & 1, (row >> 1) & 1, row >> 1
    start = jnp.where(row // ratio == feat, row % ratio * units, 1 << 20)
    where = jnp.stack([core, feat, side, turn, place, start]).astype(jnp.int32)

    def across(left, right):
        both = jnp.dot(left, right, preferred_element_type=f32).reshape(feats, part, width)
        mask = 1
        while True:
            pairs = both.reshape(both.shape[0] // 2, 2, part, width)
            bit = (feat // mask) % 2
            sent = pick(pairs, 1 - bit, 1).astype(f32 if mask == 1 else b16)
            last = 2 * mask >= feats
            kept = pick(pairs, bit, 1)
            recv = swap(sent, "feat", mask)
            mask *= 2
            if last:
                return kept[0], recv[0]
            both = kept + recv.astype(f32)

    kept_x, recv_x = across(acts, proj_in)
    kept_g, recv_g = across(grads_out, proj_out)

    ids = doc_ids.reshape(blocks, BLOCK)
    arrays = block_sums(
        row.reshape(1), where, block_counts, ids, kept_x, recv_x, kept_g, recv_g, blocks, places
    )
    arrays = [arrays[0]] + [swap(arrays[k], "rows", 2 * k) for k in range(1, places)]
    own, other = deal(where, arrays, mine)

    def diagonal(x, mask):
        pairs = [
            (f * rows + r, (f ^ mask) * rows + (r ^ 1)) for f in range(feats) for r in range(rows)
        ]
        return lax.ppermute(x, ("feat", "rows"), pairs)

    masks = range(2, feats, 2)
    got = [(0, m, diagonal(other, m)) for m in masks]
    got = got[::-1]
    crossed = {(1, m): x for _, m, x in got}
    crossed.update({(0, m): swap(own, "feat", m) for m in masks})
    crossed[1, 0] = swap(other, "rows", 1)
    crossed[0, 0] = own
    order = [(y, m) for y in (0, 1) for m in range(0, feats, 2)]
    parts = [crossed[at] for at in order] + [swap(crossed[at], "feat", 1) for at in order]

    member, counts = members(where, block_counts, units, mine, places, feats // 2, blocks)

    diag = inverse_diag.reshape(units, width)
    ready_first = fetch(where, inverse_dense, True)
    ready_second = fetch(where, inverse_dense, False)
    sent, docgrad = dense_first(where, member, counts, diag, ready_first, inverse_dense, parts, units)
    kept = dense_second(where, docgrad, diag, ready_second, inverse_dense)
    own, sent = split(where, kept, swap(sent, "rows", 1))
    own = own + swap(sent, "rows", 2).astype(f32)
    mask = 4
    while mask < rows:
        own = own + swap(own.astype(b16), "rows", mask).astype(f32)
        mask *= 2
    own = own.astype(b16)
    train_near = turned(where, train_grads, False)
    train_far = turned(where, train_grads, True)
    next_ = swap(own, "rows", 2)
    own_y = swap(own, "rows", 1)
    next_y = swap(next_, "rows", 1)
    before = score_near(where, own, next_, train_near)

    kept, sent = score_far(where, own_y, next_y, before, train_far, feats)
    scores = kept + swap(sent, "feat", 1)
    mask = 2
    while mask < feats:
        pairs = scores.reshape(scores.shape[0] // 2, 2, docs // feats, -1)
        bit = (feat // mask) % 2
        scores = pick(pairs, bit, 1) + swap(pick(pairs, 1 - bit, 1), "feat", mask)
        mask *= 2
    return scores[0]


def solution(mesh):
    in_specs = (
        P("rows", "feat"),
        P("rows", "feat"),
        P("feat", None),
        P("feat", None),
        P("rows"),
        P(),
        P("rows", "feat"),
        P("rows"),
        P("rows", "feat"),
    )
    out_specs = P("feat", "rows")
    return jax.shard_map(per_device, mesh=mesh, in_specs=in_specs, out_specs=out_specs, check_vma=False)
```

```python
import jax
import jax.numpy as jnp
from jax import lax
from jax.experimental import pallas as pl
from jax.experimental.pallas import tpu as pltpu
from jax.sharding import PartitionSpec as P


BLOCK = 128
LANES = 128
SMEM = pl.BlockSpec(memory_space=pltpu.SMEM)
VMEM = pl.BlockSpec(memory_space=pltpu.VMEM)
HBM = pl.BlockSpec(memory_space=pltpu.HBM)
_, FEAT, SIDE, TURN, PLACE, ROW = range(6)


def positions():
    row, feat = lax.axis_index("rows"), lax.axis_index("feat")
    return feat & 1, feat, row & 1, (row >> 1) & 1, row >> 1, row


def swap(x, axis, mask):
    count = lax.axis_size(axis)
    return lax.ppermute(x, axis, [(i, i ^ mask) for i in range(count)])


def pick(x, index, axis=0):
    return lax.dynamic_index_in_dim(x, index, axis, keepdims=False)


def in_hbm(x):
    return pltpu.with_memory_space_constraint(x, pltpu.HBM)


def limit(mib):
    return pltpu.CompilerParams(vmem_limit_bytes=mib << 20)


def sums_kernel(blocks, counts_ref, ids_ref, kx_ref, rx_ref, kg_ref, rg_ref, *refs):
    outs, sums_ref = refs[:-1], refs[-1]
    mine = sums_ref.shape[0]
    docs = counts_ref.shape[0]
    where_ref = positions()
    xin = (kx_ref[...] + rx_ref[...].astype(jnp.float32)).astype(jnp.bfloat16)
    gout = (kg_ref[...] + rg_ref[...].astype(jnp.float32)).astype(jnp.bfloat16)
    for j in range(mine):
        local = where_ref[FEAT] * mine + j
        block = where_ref[ROW] * blocks + local

        def count(d, carry):
            first, owner = carry
            return first + counts_ref[d], owner + (first <= block).astype(jnp.int32)

        _, owner = lax.fori_loop(0, docs, count, (jnp.int32(0), jnp.int32(-1)), unroll=True)
        keep = ids_ref[pl.ds(local, 1), :] == owner
        part = slice(j * BLOCK, (j + 1) * BLOCK)
        turned = gout[part].astype(jnp.float32).T
        masked = jnp.where(keep, turned, 0.0).astype(jnp.bfloat16)
        sums_ref[j] = jnp.dot(masked, xin[part], preferred_element_type=jnp.float32)
    few = outs[0].shape[0] // mine
    for k, out_ref in enumerate(outs):
        at = pl.multiple_of((where_ref[PLACE] ^ k) * few, few)
        for j in range(mine):
            piece = sums_ref[j, pl.ds(at, few), :]
            out_ref[j * few : (j + 1) * few] = piece.astype(out_ref.dtype)


def block_sums(counts, ids, kept_x, recv_x, kept_g, recv_g, blocks, places):
    part, width = kept_x.shape
    mine = part // BLOCK
    few = width // places
    shape = jax.ShapeDtypeStruct((mine * few, width), jnp.bfloat16)

    def kernel(*refs):
        sums_kernel(blocks, *refs)

    return pl.pallas_call(
        kernel,
        out_shape=[shape] * places,
        in_specs=[SMEM] + [VMEM] * 5,
        out_specs=[VMEM] * places,
        scratch_shapes=[pltpu.VMEM((mine, width, width), jnp.float32)],
        compiler_params=limit(8),
        name="sums",
    )(counts, ids, kept_x, recv_x, kept_g, recv_g)


def deal(arrays, mine):
    rows, width = arrays[0].shape
    shape = jax.ShapeDtypeStruct((len(arrays) * rows // 2, width), arrays[0].dtype)

    def kernel(*refs):
        where_ref = positions()
        own_ref, other_ref = refs[-2:]
        first = where_ref[SIDE] == 0
        few = rows // mine
        half = few // 2
        for k, ref in enumerate(refs[:-2]):
            got = ref[...].astype(jnp.float32)
            for j in range(mine):
                low, high = got[j * few : j * few + half], got[j * few + half : (j + 1) * few]
                at = slice((k * mine + j) * half, (k * mine + j + 1) * half)
                own_ref[at] = jnp.where(first, low, high).astype(own_ref.dtype)
                other_ref[at] = jnp.where(first, high, low).astype(own_ref.dtype)

    return pl.pallas_call(
        kernel,
        out_shape=[shape, shape],
        in_specs=[VMEM] * len(arrays),
        out_specs=[VMEM, VMEM],
        compiler_params=limit(4),
        name="deal",
    )(*arrays)


def members(counts, units, mine, places, pairs, blocks):
    docs = counts.shape[0]
    cols = units * mine * places * pairs * 4

    def kernel(counts_ref, member_ref, broad_ref):
        where_ref = positions()
        doc = lax.broadcasted_iota(jnp.int32, (docs, LANES), 0)
        starts = jnp.zeros((docs, LANES), jnp.int32)
        broad = jnp.zeros((docs, LANES), jnp.int32)
        for d in range(docs):
            starts += jnp.where(doc > d, counts_ref[d], 0)
            broad += jnp.where(doc == d, counts_ref[d], 0)
        broad_ref[...] = broad.astype(jnp.float32)
        ends = starts + broad
        side, place, feat = where_ref[SIDE], where_ref[PLACE], where_ref[FEAT]
        for n in range(cols // LANES):
            col = lax.broadcasted_iota(jnp.int32, (docs, LANES), 1) + n * LANES
            at, cut = [], col
            for size in (units, mine, places, pairs, 2, 2):
                bits = size.bit_length() - 1
                at.append(cut & (size - 1))
                cut = lax.shift_right_logical(cut, bits)
            unit, j, k, x, y, c = at
            from_row = 2 * (place ^ k) + (side ^ y)
            which = from_row * blocks + (feat ^ (2 * x) ^ c) * mine + j
            holds = (starts <= which) & (which < ends)
            for u in range(units):
                part = jnp.where(holds & (unit == u), 1.0, 0.0).astype(jnp.bfloat16)
                member_ref[u * docs : (u + 1) * docs, n * LANES : (n + 1) * LANES] = part

    return pl.pallas_call(
        kernel,
        out_shape=[
            jax.ShapeDtypeStruct((units * docs, cols), jnp.bfloat16),
            jax.ShapeDtypeStruct((docs, LANES), jnp.float32),
        ],
        in_specs=[SMEM],
        out_specs=[VMEM, VMEM],
        compiler_params=limit(4),
        name="members",
    )(counts)


def begin(source_ref, base, held_ref, sems):
    tile = held_ref.shape[1] // sems.shape[0]
    copies = []
    for n in range(sems.shape[0]):
        at = pl.multiple_of(base + n * tile, tile)
        place = held_ref.at[:, pl.ds(n * tile, tile)]
        copies.append(pltpu.make_async_copy(source_ref.at[:, pl.ds(at, tile)], place, sems.at[n]))
    for copy in copies:
        copy.start()
    return copies


def fetch(inverse, other):
    depth, cols = inverse.shape
    quarter = cols // 4

    def kernel(source_ref, out_ref, sems):
        where_ref = positions()
        half = 1 - where_ref[SIDE] if other else where_ref[SIDE]
        for copy in begin(source_ref, half * 2 * quarter, out_ref, sems):
            copy.wait()

    return pl.pallas_call(
        kernel,
        out_shape=jax.ShapeDtypeStruct((depth, quarter), inverse.dtype),
        in_specs=[HBM],
        out_specs=VMEM,
        scratch_shapes=[pltpu.SemaphoreType.DMA((tiles(quarter),))],
        compiler_params=limit(6),
        name="fetch",
    )(in_hbm(inverse))


def tiles(quarter):
    return max(quarter // 512, 1)


def dense_body(make_left, grad_ref, diag_ref, ready_ref, source_ref, out_ref, held_ref, sems, half):
    units = grad_ref.shape[0]
    quarter = out_ref.shape[2]
    steps = sems.shape[0]
    tile = quarter // steps
    copies = begin(source_ref, (2 * half + 1) * quarter, held_ref, sems)
    ratio = lax.axis_size("rows") // lax.axis_size("feat")
    row, feat = lax.axis_index("rows"), lax.axis_index("feat")
    start = jnp.where(row // ratio == feat, row % ratio * units, 1 << 20)
    left = make_left()
    for piece in range(2):
        for n in range(steps):
            col = n * tile
            if piece:
                copies[n].wait()
            ref = held_ref if piece else ready_ref
            total = jnp.dot(left, ref[:, col : col + tile], preferred_element_type=jnp.float32)
            out_ref[piece, :, col : col + tile] = total.astype(out_ref.dtype)
            base = (2 * half + piece) * quarter + col
            for q in range(tile // LANES):
                unit = base // LANES + q - start

                @pl.when((unit >= 0) & (unit < units))
                def _():
                    a = jnp.clip(unit, 0, units - 1)
                    term = grad_ref[a].astype(jnp.float32) * diag_ref[pl.ds(a, 1), :]
                    part = total[:, q * LANES : (q + 1) * LANES] + term
                    cols = slice(col + q * LANES, col + (q + 1) * LANES)
                    out_ref[piece, :, cols] = part.astype(out_ref.dtype)


def joined(grad_ref):
    return jnp.concatenate([grad_ref[u] for u in range(grad_ref.shape[0])], axis=1)


def first_kernel(member_ref, counts_ref, diag_ref, ready_ref, source_ref, *refs):
    arrays, (out_ref, grad_ref, held_ref, sems) = refs[:-4], refs[-4:]
    units, docs, _ = grad_ref.shape
    each = arrays[0].shape[0]

    def make_left():
        summed = None
        for s, ref in enumerate(arrays):
            part = jnp.dot(
                member_ref[:, s * each : (s + 1) * each],
                ref[...],
                preferred_element_type=jnp.float32,
            )
            summed = part if summed is None else summed + part
        for u in range(units):
            mean = summed[u * docs : (u + 1) * docs] / counts_ref[...]
            grad_ref[u] = mean.astype(grad_ref.dtype)
        return joined(grad_ref)

    half = 1 - positions()[SIDE]
    dense_body(
        make_left, grad_ref, diag_ref, ready_ref, source_ref, out_ref, held_ref, sems, half
    )


def held_scratch(inverse):
    quarter = inverse.shape[1] // 4
    return [
        pltpu.VMEM((inverse.shape[0], quarter), inverse.dtype),
        pltpu.SemaphoreType.DMA((tiles(quarter),)),
    ]


def dense_first(member, counts, diag, ready, inverse, arrays, units):
    docs = counts.shape[0]
    return pl.pallas_call(
        first_kernel,
        out_shape=[
            jax.ShapeDtypeStruct((2, docs, inverse.shape[1] // 4), jnp.bfloat16),
            jax.ShapeDtypeStruct((units, docs, LANES), jnp.bfloat16),
        ],
        in_specs=[VMEM] * 4 + [HBM] + [VMEM] * len(arrays),
        out_specs=[VMEM, VMEM],
        scratch_shapes=held_scratch(inverse),
        compiler_params=limit(16),
        name="first",
    )(member, counts, diag, ready, in_hbm(inverse), *arrays)


def second_kernel(grad_ref, diag_ref, ready_ref, source_ref, out_ref, held_ref, sems):
    make_left = lambda: joined(grad_ref)
    half = positions()[SIDE]
    dense_body(
        make_left, grad_ref, diag_ref, ready_ref, source_ref, out_ref, held_ref, sems, half
    )


def dense_second(docgrad, diag, ready, inverse):
    docs = docgrad.shape[1]
    return pl.pallas_call(
        second_kernel,
        out_shape=jax.ShapeDtypeStruct((2, docs, inverse.shape[1] // 4), jnp.float32),
        in_specs=[VMEM] * 3 + [HBM],
        out_specs=VMEM,
        scratch_shapes=held_scratch(inverse),
        compiler_params=limit(16),
        name="second",
    )(docgrad, diag, ready, in_hbm(inverse))


def split_kernel(kept_ref, recv_ref, own_ref, sent_ref):
    turn = positions()[TURN]
    own_ref[...] = kept_ref[turn] + recv_ref[turn].astype(jnp.float32)
    sent = kept_ref[1 - turn] + recv_ref[1 - turn].astype(jnp.float32)
    sent_ref[...] = sent.astype(sent_ref.dtype)


def split(kept, recv):
    shape = kept.shape[1:]
    return pl.pallas_call(
        split_kernel,
        out_shape=[
            jax.ShapeDtypeStruct(shape, jnp.float32),
            jax.ShapeDtypeStruct(shape, jnp.bfloat16),
        ],
        in_specs=[VMEM, VMEM],
        out_specs=[VMEM, VMEM],
        compiler_params=limit(4),
        name="split",
    )(kept, recv)


def turned(train, other):
    count, cols = train.shape
    half = cols // 2
    steps = 4
    tile = half // steps

    def kernel(source_ref, out_ref, held_ref, sems):
        where_ref = positions()
        which = 1 - where_ref[SIDE] if other else where_ref[SIDE]
        copies = []
        for n in range(steps):
            at = pl.multiple_of(which * half + n * tile, tile)
            place = held_ref.at[:, pl.ds(n * tile, tile)]
            copies.append(pltpu.make_async_copy(source_ref.at[:, pl.ds(at, tile)], place, sems.at[n]))
        for copy in copies:
            copy.start()
        for n in range(steps):
            copies[n].wait()
            part = slice(n * tile, (n + 1) * tile)
            out_ref[part, :] = held_ref[:, part].T

    return pl.pallas_call(
        kernel,
        out_shape=jax.ShapeDtypeStruct((half, count), train.dtype),
        in_specs=[HBM],
        out_specs=VMEM,
        scratch_shapes=[
            pltpu.VMEM((count, half), train.dtype),
            pltpu.SemaphoreType.DMA((steps,)),
        ],
        compiler_params=limit(8),
        name="turned",
    )(in_hbm(train))


def score_part(ref, train_ref, shift):
    quarter = ref.shape[1]
    at = pl.multiple_of((positions()[TURN] ^ shift) * quarter, quarter)
    return jnp.dot(ref[...], train_ref[pl.ds(at, quarter), :], preferred_element_type=jnp.float32)


def score_near(near, far, train):
    def kernel(near_ref, far_ref, train_ref, out_ref):
        out_ref[...] = score_part(near_ref, train_ref, 0) + score_part(far_ref, train_ref, 1)

    return pl.pallas_call(
        kernel,
        out_shape=jax.ShapeDtypeStruct((near.shape[0], train.shape[1]), jnp.float32),
        in_specs=[VMEM] * 3,
        out_specs=VMEM,
        compiler_params=limit(4),
        name="near",
    )(near, far, train)


def score_beside(near, before, train):
    def kernel(near_ref, before_ref, train_ref, out_ref):
        out_ref[...] = before_ref[...] + score_part(near_ref, train_ref, 0)

    return pl.pallas_call(
        kernel,
        out_shape=jax.ShapeDtypeStruct(before.shape, jnp.float32),
        in_specs=[VMEM] * 3,
        out_specs=VMEM,
        compiler_params=limit(4),
        name="beside",
    )(near, before, train)


def score_far(far, before, train, feats):
    docs, count = before.shape
    few = docs // feats
    shape = jax.ShapeDtypeStruct((few, count), jnp.float32)

    def kernel(far_ref, before_ref, train_ref, *refs):
        outs, all_ref = refs[:-1], refs[-1]
        all_ref[...] = before_ref[...] + score_part(far_ref, train_ref, 1)
        for m, ref in enumerate(outs):
            at = pl.multiple_of((positions()[FEAT] ^ m) * few, few)
            ref[...] = all_ref[pl.ds(at, few), :]

    return pl.pallas_call(
        kernel,
        out_shape=[shape] * feats,
        in_specs=[VMEM] * 3,
        out_specs=[VMEM] * feats,
        scratch_shapes=[pltpu.VMEM((docs, count), jnp.float32)],
        compiler_params=limit(4),
        name="far",
    )(far, before, train)


def per_device(
    acts,
    grads_out,
    proj_in,
    proj_out,
    doc_ids,
    block_counts,
    inverse_dense,
    inverse_diag,
    train_grads,
):
    tokens = acts.shape[0]
    rows = lax.axis_size("rows")
    feats = lax.axis_size("feat")
    feat = lax.axis_index("feat")
    width = proj_in.shape[1]
    part = tokens // feats
    mine = part // BLOCK
    blocks = tokens // BLOCK
    units = width // rows
    places = rows // 2
    f32, b16 = jnp.float32, jnp.bfloat16

    def across(left, right):
        both = jnp.dot(left, right, preferred_element_type=f32).reshape(feats, part, width)
        mask = 1
        while True:
            pairs = both.reshape(both.shape[0] // 2, 2, part, width)
            bit = (feat // mask) % 2
            sent = pick(pairs, 1 - bit, 1).astype(f32 if mask == 1 else b16)
            last = 2 * mask >= feats
            kept = pick(pairs, bit, 1)
            recv = swap(sent, "feat", mask)
            mask *= 2
            if last:
                return kept[0], recv[0]
            both = kept + recv.astype(f32)

    kept_x, recv_x = across(acts, proj_in)
    kept_g, recv_g = across(grads_out, proj_out)

    ids = doc_ids.reshape(blocks, BLOCK)
    arrays = block_sums(
        block_counts, ids, kept_x, recv_x, kept_g, recv_g, blocks, places
    )
    arrays = [arrays[0]] + [swap(arrays[k], "rows", 2 * k) for k in range(1, places)]
    own, other = deal(arrays, mine)

    def diagonal(x, mask):
        pairs = [
            (f * rows + r, (f ^ mask) * rows + (r ^ 1)) for f in range(feats) for r in range(rows)
        ]
        return lax.ppermute(x, ("feat", "rows"), pairs)

    masks = range(2, feats, 2)
    got = [(0, m, diagonal(other, m)) for m in masks]
    got = got[::-1]
    crossed = {(1, m): x for _, m, x in got}
    crossed.update({(0, m): swap(own, "feat", m) for m in masks})
    crossed[1, 0] = swap(other, "rows", 1)
    crossed[0, 0] = own
    order = [(y, m) for y in (0, 1) for m in range(0, feats, 2)]
    parts = [crossed[at] for at in order] + [swap(crossed[at], "feat", 1) for at in order]

    member, counts = members(block_counts, units, mine, places, feats // 2, blocks)

    diag = inverse_diag.reshape(units, width)
    ready_first = fetch(inverse_dense, True)
    ready_second = fetch(inverse_dense, False)
    sent, docgrad = dense_first(member, counts, diag, ready_first, inverse_dense, parts, units)
    kept = dense_second(docgrad, diag, ready_second, inverse_dense)
    own, sent = split(kept, swap(sent, "rows", 1))
    own = own + swap(sent, "rows", 2).astype(f32)
    mask = 4
    while mask < rows:
        own = own + swap(own.astype(b16), "rows", mask).astype(f32)
        mask *= 2
    own = own.astype(b16)
    train_near = turned(train_grads, False)
    train_far = turned(train_grads, True)
    next_ = swap(own, "rows", 2)
    own_y = swap(own, "rows", 1)
    next_y = swap(next_, "rows", 1)
    before = score_near(own, next_, train_near)
    before = score_beside(own_y, before, train_far)

    pieces = score_far(next_y, before, train_far, feats)
    arrived = [swap(pieces[m], "feat", m) for m in range(feats - 1, 0, -1)]
    scores = pieces[0]
    for piece in arrived:
        scores = scores + piece
    return scores


def solution(mesh):
    in_specs = (
        P("rows", "feat"),
        P("rows", "feat"),
        P("feat", None),
        P("feat", None),
        P("rows"),
        P(),
        P("rows", "feat"),
        P("rows"),
        P("rows", "feat"),
    )
    out_specs = P("feat", "rows")
    return jax.shard_map(per_device, mesh=mesh, in_specs=in_specs, out_specs=out_specs, check_vma=False)
```

```python
import jax
import jax.numpy as jnp
from jax import lax
from jax.experimental import pallas as pl
from jax.experimental.pallas import tpu as pltpu
from jax.sharding import PartitionSpec as P


BLOCK = 128
LANES = 128
SMEM = pl.BlockSpec(memory_space=pltpu.SMEM)
VMEM = pl.BlockSpec(memory_space=pltpu.VMEM)
HBM = pl.BlockSpec(memory_space=pltpu.HBM)
_, FEAT, SIDE, TURN, PLACE, ROW = range(6)


def positions():
    row, feat = lax.axis_index("rows"), lax.axis_index("feat")
    return feat & 1, feat, row & 1, (row >> 1) & 1, row >> 1, row


def swap(x, axis, mask):
    count = lax.axis_size(axis)
    return lax.ppermute(x, axis, [(i, i ^ mask) for i in range(count)])


def pick(x, index, axis=0):
    return lax.dynamic_index_in_dim(x, index, axis, keepdims=False)


def in_hbm(x):
    return pltpu.with_memory_space_constraint(x, pltpu.HBM)


def limit(mib):
    return pltpu.CompilerParams(vmem_limit_bytes=mib << 20)


def sums_kernel(blocks, counts_ref, ids_ref, kx_ref, rx_ref, kg_ref, rg_ref, *refs):
    outs, sums_ref = refs[:-1], refs[-1]
    mine = sums_ref.shape[0]
    docs = counts_ref.shape[0]
    where_ref = positions()
    xin = (kx_ref[...] + rx_ref[...].astype(jnp.float32)).astype(jnp.bfloat16)
    gout = (kg_ref[...] + rg_ref[...].astype(jnp.float32)).astype(jnp.bfloat16)
    for j in range(mine):
        local = where_ref[FEAT] * mine + j
        block = where_ref[ROW] * blocks + local

        def count(d, carry):
            first, owner = carry
            return first + counts_ref[d], owner + (first <= block).astype(jnp.int32)

        _, owner = lax.fori_loop(0, docs, count, (jnp.int32(0), jnp.int32(-1)), unroll=True)
        keep = ids_ref[pl.ds(local, 1), :] == owner
        part = slice(j * BLOCK, (j + 1) * BLOCK)
        turned = gout[part].astype(jnp.float32).T
        masked = jnp.where(keep, turned, 0.0).astype(jnp.bfloat16)
        sums_ref[j] = jnp.dot(masked, xin[part], preferred_element_type=jnp.float32)
    few = outs[0].shape[0] // mine
    for k, out_ref in enumerate(outs):
        at = pl.multiple_of((where_ref[PLACE] ^ k) * few, few)
        for j in range(mine):
            piece = sums_ref[j, pl.ds(at, few), :]
            out_ref[j * few : (j + 1) * few] = piece.astype(out_ref.dtype)


def block_sums(counts, ids, kept_x, recv_x, kept_g, recv_g, blocks, places):
    part, width = kept_x.shape
    mine = part // BLOCK
    few = width // places
    shape = jax.ShapeDtypeStruct((mine * few, width), jnp.bfloat16)

    def kernel(*refs):
        sums_kernel(blocks, *refs)

    return pl.pallas_call(
        kernel,
        out_shape=[shape] * places,
        in_specs=[SMEM] + [VMEM] * 5,
        out_specs=[VMEM] * places,
        scratch_shapes=[pltpu.VMEM((mine, width, width), jnp.float32)],
        compiler_params=limit(8),
        name="sums",
    )(counts, ids, kept_x, recv_x, kept_g, recv_g)


def deal(arrays, mine):
    rows, width = arrays[0].shape
    shape = jax.ShapeDtypeStruct((len(arrays) * rows // 2, width), arrays[0].dtype)

    def kernel(*refs):
        where_ref = positions()
        own_ref, other_ref = refs[-2:]
        first = where_ref[SIDE] == 0
        few = rows // mine
        half = few // 2
        for k, ref in enumerate(refs[:-2]):
            got = ref[...].astype(jnp.float32)
            for j in range(mine):
                low, high = got[j * few : j * few + half], got[j * few + half : (j + 1) * few]
                at = slice((k * mine + j) * half, (k * mine + j + 1) * half)
                own_ref[at] = jnp.where(first, low, high).astype(own_ref.dtype)
                other_ref[at] = jnp.where(first, high, low).astype(own_ref.dtype)

    return pl.pallas_call(
        kernel,
        out_shape=[shape, shape],
        in_specs=[VMEM] * len(arrays),
        out_specs=[VMEM, VMEM],
        compiler_params=limit(4),
        name="deal",
    )(*arrays)


def members(counts, units, mine, places, pairs, blocks):
    docs = counts.shape[0]
    cols = units * mine * places * pairs * 4

    def kernel(counts_ref, member_ref, broad_ref):
        where_ref = positions()
        doc = lax.broadcasted_iota(jnp.int32, (docs, LANES), 0)
        starts = jnp.zeros((docs, LANES), jnp.int32)
        broad = jnp.zeros((docs, LANES), jnp.int32)
        for d in range(docs):
            starts += jnp.where(doc > d, counts_ref[d], 0)
            broad += jnp.where(doc == d, counts_ref[d], 0)
        broad_ref[...] = broad.astype(jnp.float32)
        ends = starts + broad
        side, place, feat = where_ref[SIDE], where_ref[PLACE], where_ref[FEAT]
        for n in range(cols // LANES):
            col = lax.broadcasted_iota(jnp.int32, (docs, LANES), 1) + n * LANES
            at, cut = [], col
            for size in (units, mine, places, pairs, 2, 2):
                bits = size.bit_length() - 1
                at.append(cut & (size - 1))
                cut = lax.shift_right_logical(cut, bits)
            unit, j, k, x, y, c = at
            from_row = 2 * (place ^ k) + (side ^ y)
            which = from_row * blocks + (feat ^ (2 * x) ^ c) * mine + j
            holds = (starts <= which) & (which < ends)
            for u in range(units):
                part = jnp.where(holds & (unit == u), 1.0, 0.0).astype(jnp.bfloat16)
                member_ref[u * docs : (u + 1) * docs, n * LANES : (n + 1) * LANES] = part

    return pl.pallas_call(
        kernel,
        out_shape=[
            jax.ShapeDtypeStruct((units * docs, cols), jnp.bfloat16),
            jax.ShapeDtypeStruct((docs, LANES), jnp.float32),
        ],
        in_specs=[SMEM],
        out_specs=[VMEM, VMEM],
        compiler_params=limit(4),
        name="members",
    )(counts)


def begin(source_ref, base, held_ref, sems):
    tile = held_ref.shape[1] // sems.shape[0]
    copies = []
    for n in range(sems.shape[0]):
        at = pl.multiple_of(base + n * tile, tile)
        place = held_ref.at[:, pl.ds(n * tile, tile)]
        copies.append(pltpu.make_async_copy(source_ref.at[:, pl.ds(at, tile)], place, sems.at[n]))
    for copy in copies:
        copy.start()
    return copies


def quarter_of(side, turn):
    at = positions()
    return 2 * (at[SIDE] ^ side) + (at[TURN] ^ turn)


def fetch(inverse, side, turn):
    depth, cols = inverse.shape
    quarter = cols // 4

    def kernel(source_ref, out_ref, sems):
        for copy in begin(source_ref, quarter_of(side, turn) * quarter, out_ref, sems):
            copy.wait()

    return pl.pallas_call(
        kernel,
        out_shape=jax.ShapeDtypeStruct((depth, quarter), inverse.dtype),
        in_specs=[HBM],
        out_specs=VMEM,
        scratch_shapes=[pltpu.SemaphoreType.DMA((tiles(quarter),))],
        compiler_params=limit(6),
        name="fetch",
    )(in_hbm(inverse))


def tiles(quarter):
    return max(quarter // 512, 1)


def dense_body(left, grad_ref, diag_ref, ready_ref, copies, out_ref, side, turn):
    units = grad_ref.shape[0]
    quarter = out_ref.shape[1]
    steps = tiles(quarter)
    tile = quarter // steps
    ratio = lax.axis_size("rows") // lax.axis_size("feat")
    row, feat = lax.axis_index("rows"), lax.axis_index("feat")
    start = jnp.where(row // ratio == feat, row % ratio * units, 1 << 20)
    for n in range(steps):
        col = n * tile
        if copies:
            copies[n].wait()
        total = jnp.dot(left, ready_ref[:, col : col + tile], preferred_element_type=jnp.float32)
        out_ref[:, col : col + tile] = total.astype(out_ref.dtype)
        for q in range(tile // LANES):
            unit = (quarter_of(side, turn) * quarter + col) // LANES + q - start

            @pl.when((unit >= 0) & (unit < units))
            def _():
                a = jnp.clip(unit, 0, units - 1)
                term = grad_ref[a].astype(jnp.float32) * diag_ref[pl.ds(a, 1), :]
                part = total[:, q * LANES : (q + 1) * LANES] + term
                cols = slice(col + q * LANES, col + (q + 1) * LANES)
                out_ref[:, cols] = part.astype(out_ref.dtype)


def joined(grad_ref):
    return jnp.concatenate([grad_ref[u] for u in range(grad_ref.shape[0])], axis=1)


def dense_first(member, counts, diag, ready, arrays, units, side, turn):
    docs = counts.shape[0]

    def kernel(member_ref, counts_ref, diag_ref, ready_ref, *refs):
        given, (out_ref, grad_ref) = refs[:-2], refs[-2:]
        each = given[0].shape[0]
        summed = None
        for s, ref in enumerate(given):
            part = jnp.dot(
                member_ref[:, s * each : (s + 1) * each],
                ref[...],
                preferred_element_type=jnp.float32,
            )
            summed = part if summed is None else summed + part
        for u in range(units):
            mean = summed[u * docs : (u + 1) * docs] / counts_ref[...]
            grad_ref[u] = mean.astype(grad_ref.dtype)
        dense_body(joined(grad_ref), grad_ref, diag_ref, ready_ref, None, out_ref, side, turn)

    return pl.pallas_call(
        kernel,
        out_shape=[
            jax.ShapeDtypeStruct((docs, ready.shape[1]), jnp.bfloat16),
            jax.ShapeDtypeStruct((units, docs, LANES), jnp.bfloat16),
        ],
        in_specs=[VMEM] * (4 + len(arrays)),
        out_specs=[VMEM, VMEM],
        compiler_params=limit(8),
        name="first",
    )(member, counts, diag, ready, *arrays)


def dense_ready(docgrad, diag, ready, side, turn):
    def kernel(grad_ref, diag_ref, ready_ref, out_ref):
        dense_body(joined(grad_ref), grad_ref, diag_ref, ready_ref, None, out_ref, side, turn)

    return pl.pallas_call(
        kernel,
        out_shape=jax.ShapeDtypeStruct((docgrad.shape[1], ready.shape[1]), jnp.bfloat16),
        in_specs=[VMEM] * 3,
        out_specs=VMEM,
        compiler_params=limit(8),
        name="ready",
    )(docgrad, diag, ready)


def dense_own(docgrad, diag, inverse):
    depth, cols = inverse.shape
    quarter = cols // 4

    def kernel(grad_ref, diag_ref, source_ref, out_ref, held_ref, sems):
        copies = begin(source_ref, quarter_of(0, 0) * quarter, held_ref, sems)
        dense_body(joined(grad_ref), grad_ref, diag_ref, held_ref, copies, out_ref, 0, 0)

    return pl.pallas_call(
        kernel,
        out_shape=jax.ShapeDtypeStruct((docgrad.shape[1], quarter), jnp.float32),
        in_specs=[VMEM, VMEM, HBM],
        out_specs=VMEM,
        scratch_shapes=[
            pltpu.VMEM((depth, quarter), inverse.dtype),
            pltpu.SemaphoreType.DMA((tiles(quarter),)),
        ],
        compiler_params=limit(12),
        name="own",
    )(docgrad, diag, in_hbm(inverse))


def turned(train, other):
    count, cols = train.shape
    half = cols // 2
    steps = 4
    tile = half // steps

    def kernel(source_ref, out_ref, held_ref, sems):
        where_ref = positions()
        which = 1 - where_ref[SIDE] if other else where_ref[SIDE]
        copies = []
        for n in range(steps):
            at = pl.multiple_of(which * half + n * tile, tile)
            place = held_ref.at[:, pl.ds(n * tile, tile)]
            copies.append(pltpu.make_async_copy(source_ref.at[:, pl.ds(at, tile)], place, sems.at[n]))
        for copy in copies:
            copy.start()
        for n in range(steps):
            copies[n].wait()
            part = slice(n * tile, (n + 1) * tile)
            out_ref[part, :] = held_ref[:, part].T

    return pl.pallas_call(
        kernel,
        out_shape=jax.ShapeDtypeStruct((half, count), train.dtype),
        in_specs=[HBM],
        out_specs=VMEM,
        scratch_shapes=[
            pltpu.VMEM((count, half), train.dtype),
            pltpu.SemaphoreType.DMA((steps,)),
        ],
        compiler_params=limit(8),
        name="turned",
    )(in_hbm(train))


def score_part(ref, train_ref, shift):
    quarter = ref.shape[1]
    at = pl.multiple_of((positions()[TURN] ^ shift) * quarter, quarter)
    return jnp.dot(ref[...], train_ref[pl.ds(at, quarter), :], preferred_element_type=jnp.float32)


def score_near(near, far, train):
    def kernel(near_ref, far_ref, train_ref, out_ref):
        out_ref[...] = score_part(near_ref, train_ref, 0) + score_part(far_ref, train_ref, 1)

    return pl.pallas_call(
        kernel,
        out_shape=jax.ShapeDtypeStruct((near.shape[0], train.shape[1]), jnp.float32),
        in_specs=[VMEM] * 3,
        out_specs=VMEM,
        compiler_params=limit(4),
        name="near",
    )(near, far, train)


def score_beside(near, before, train):
    def kernel(near_ref, before_ref, train_ref, out_ref):
        out_ref[...] = before_ref[...] + score_part(near_ref, train_ref, 0)

    return pl.pallas_call(
        kernel,
        out_shape=jax.ShapeDtypeStruct(before.shape, jnp.float32),
        in_specs=[VMEM] * 3,
        out_specs=VMEM,
        compiler_params=limit(4),
        name="beside",
    )(near, before, train)


def score_far(far, before, train, feats):
    docs, count = before.shape
    few = docs // feats
    shape = jax.ShapeDtypeStruct((few, count), jnp.float32)

    def kernel(far_ref, before_ref, train_ref, *refs):
        outs, all_ref = refs[:-1], refs[-1]
        all_ref[...] = before_ref[...] + score_part(far_ref, train_ref, 1)
        for m, ref in enumerate(outs):
            at = pl.multiple_of((positions()[FEAT] ^ m) * few, few)
            ref[...] = all_ref[pl.ds(at, few), :]

    return pl.pallas_call(
        kernel,
        out_shape=[shape] * feats,
        in_specs=[VMEM] * 3,
        out_specs=[VMEM] * feats,
        scratch_shapes=[pltpu.VMEM((docs, count), jnp.float32)],
        compiler_params=limit(4),
        name="far",
    )(far, before, train)


def per_device(
    acts,
    grads_out,
    proj_in,
    proj_out,
    doc_ids,
    block_counts,
    inverse_dense,
    inverse_diag,
    train_grads,
):
    tokens = acts.shape[0]
    rows = lax.axis_size("rows")
    feats = lax.axis_size("feat")
    feat = lax.axis_index("feat")
    width = proj_in.shape[1]
    part = tokens // feats
    mine = part // BLOCK
    blocks = tokens // BLOCK
    units = width // rows
    places = rows // 2
    f32, b16 = jnp.float32, jnp.bfloat16

    def across(left, right):
        both = jnp.dot(left, right, preferred_element_type=f32).reshape(feats, part, width)
        mask = 1
        while True:
            pairs = both.reshape(both.shape[0] // 2, 2, part, width)
            bit = (feat // mask) % 2
            sent = pick(pairs, 1 - bit, 1).astype(f32 if mask == 1 else b16)
            last = 2 * mask >= feats
            kept = pick(pairs, bit, 1)
            recv = swap(sent, "feat", mask)
            mask *= 2
            if last:
                return kept[0], recv[0]
            both = kept + recv.astype(f32)

    kept_x, recv_x = across(acts, proj_in)
    kept_g, recv_g = across(grads_out, proj_out)

    ids = doc_ids.reshape(blocks, BLOCK)
    arrays = block_sums(
        block_counts, ids, kept_x, recv_x, kept_g, recv_g, blocks, places
    )
    arrays = [arrays[0]] + [swap(arrays[k], "rows", 2 * k) for k in range(1, places)]
    own, other = deal(arrays, mine)

    def diagonal(x, mask):
        pairs = [
            (f * rows + r, (f ^ mask) * rows + (r ^ 1)) for f in range(feats) for r in range(rows)
        ]
        return lax.ppermute(x, ("feat", "rows"), pairs)

    masks = range(2, feats, 2)
    got = [(0, m, diagonal(other, m)) for m in masks]
    got = got[::-1]
    crossed = {(1, m): x for _, m, x in got}
    crossed.update({(0, m): swap(own, "feat", m) for m in masks})
    crossed[1, 0] = swap(other, "rows", 1)
    crossed[0, 0] = own
    order = [(y, m) for y in (0, 1) for m in range(0, feats, 2)]
    parts = [crossed[at] for at in order] + [swap(crossed[at], "feat", 1) for at in order]

    member, counts = members(block_counts, units, mine, places, feats // 2, blocks)

    diag = inverse_diag.reshape(units, width)
    ready_both = fetch(inverse_dense, 1, 1)
    ready_side = fetch(inverse_dense, 1, 0)
    ready_turn = fetch(inverse_dense, 0, 1)
    part, docgrad = dense_first(member, counts, diag, ready_both, parts, units, 1, 1)
    part_both = swap(part, "rows", 3)
    part = dense_ready(docgrad, diag, ready_side, 1, 0)
    part_side = swap(part, "rows", 1)
    part = dense_ready(docgrad, diag, ready_turn, 0, 1)
    part_turn = swap(part, "rows", 2)
    own = dense_own(docgrad, diag, inverse_dense)
    own = own + part_both.astype(f32) + part_side.astype(f32) + part_turn.astype(f32)
    mask = 4
    while mask < rows:
        own = own + swap(own.astype(b16), "rows", mask).astype(f32)
        mask *= 2
    own = own.astype(b16)
    train_near = turned(train_grads, False)
    train_far = turned(train_grads, True)
    own_both = swap(own, "rows", 3)
    own_side = swap(own, "rows", 1)
    own_turn = swap(own, "rows", 2)
    before = score_near(own, own_turn, train_near)
    before = score_beside(own_side, before, train_far)

    pieces = score_far(own_both, before, train_far, feats)
    arrived = [swap(pieces[m], "feat", m) for m in range(feats - 1, 0, -1)]
    scores = pieces[0]
    for piece in arrived:
        scores = scores + piece
    return scores


def solution(mesh):
    in_specs = (
        P("rows", "feat"),
        P("rows", "feat"),
        P("feat", None),
        P("feat", None),
        P("rows"),
        P(),
        P("rows", "feat"),
        P("rows"),
        P("rows", "feat"),
    )
    out_specs = P("feat", "rows")
    return jax.shard_map(per_device, mesh=mesh, in_specs=in_specs, out_specs=out_specs, check_vma=False)
```

```python
import jax
import jax.numpy as jnp
from jax import lax
from jax.experimental import pallas as pl
from jax.experimental.pallas import tpu as pltpu
from jax.sharding import PartitionSpec as P


BLOCK = 128
LANES = 128
SMEM = pl.BlockSpec(memory_space=pltpu.SMEM)
VMEM = pl.BlockSpec(memory_space=pltpu.VMEM)
HBM = pl.BlockSpec(memory_space=pltpu.HBM)
ROWS, FEATS = "rows", "feat"
_, FEAT, SIDE, TURN, PLACE, ROW = range(6)


def positions():
    row, feat = lax.axis_index(ROWS), lax.axis_index(FEATS)
    return feat & 1, feat, row & 1, (row >> 1) & 1, row >> 1, row


def swap(x, axis, mask):
    count = lax.axis_size(axis)
    return lax.ppermute(x, axis, [(i, i ^ mask) for i in range(count)])


def pick(x, index, axis=0):
    return lax.dynamic_index_in_dim(x, index, axis, keepdims=False)


def in_hbm(x):
    return pltpu.with_memory_space_constraint(x, pltpu.HBM)


def limit(mib):
    return pltpu.CompilerParams(vmem_limit_bytes=mib << 20)


def sums_kernel(keep_ref, kx_ref, rx_ref, kg_ref, rg_ref, *refs):
    outs, sums_ref = refs[:-1], refs[-1]
    mine = sums_ref.shape[0]
    where_ref = positions()
    xin = (kx_ref[...] + rx_ref[...].astype(jnp.float32)).astype(jnp.bfloat16)
    gout = (kg_ref[...] + rg_ref[...].astype(jnp.float32)).astype(jnp.bfloat16)
    for j in range(mine):
        part = slice(j * BLOCK, (j + 1) * BLOCK)
        flipped = gout[part].astype(jnp.float32).T
        masked = jnp.where(keep_ref[j : j + 1, :] > 0.0, flipped, 0.0).astype(jnp.bfloat16)
        sums_ref[j] = jnp.dot(masked, xin[part], preferred_element_type=jnp.float32)
    few = outs[0].shape[0] // mine
    for k, out_ref in enumerate(outs):
        at = pl.multiple_of((where_ref[PLACE] ^ k) * few, few)
        for j in range(mine):
            piece = sums_ref[j, pl.ds(at, few), :]
            out_ref[j * few : (j + 1) * few] = piece.astype(out_ref.dtype)


def block_sums(keep, kept_x, recv_x, kept_g, recv_g, places):
    part, width = kept_x.shape
    mine = part // BLOCK
    few = width // places
    shape = jax.ShapeDtypeStruct((mine * few, width), jnp.bfloat16)
    return pl.pallas_call(
        sums_kernel,
        out_shape=[shape] * places,
        in_specs=[VMEM] * 5,
        out_specs=[VMEM] * places,
        scratch_shapes=[pltpu.VMEM((mine, width, width), jnp.float32)],
        compiler_params=limit(8),
    )(keep, kept_x, recv_x, kept_g, recv_g)


def deal(arrays, mine):
    rows, width = arrays[0].shape
    shape = jax.ShapeDtypeStruct((len(arrays) * rows // 2, width), arrays[0].dtype)

    def kernel(*refs):
        where_ref = positions()
        own_ref, other_ref = refs[-2:]
        first = where_ref[SIDE] == 0
        few = rows // mine
        half = few // 2
        for k, ref in enumerate(refs[:-2]):
            got = ref[...].astype(jnp.float32)
            for j in range(mine):
                low, high = got[j * few : j * few + half], got[j * few + half : (j + 1) * few]
                at = slice((k * mine + j) * half, (k * mine + j + 1) * half)
                own_ref[at] = jnp.where(first, low, high).astype(own_ref.dtype)
                other_ref[at] = jnp.where(first, high, low).astype(own_ref.dtype)

    return pl.pallas_call(
        kernel,
        out_shape=[shape, shape],
        in_specs=[VMEM] * len(arrays),
        out_specs=[VMEM, VMEM],
        compiler_params=limit(4),
    )(*arrays)


def members(counts, ids, units, mine, places, pairs, blocks):
    docs = counts.shape[0]
    cols = units * mine * places * pairs * 4

    def kernel(counts_ref, ids_ref, member_ref, broad_ref, keep_ref):
        where_ref = positions()
        for j in range(mine):
            local = where_ref[FEAT] * mine + j
            block = where_ref[ROW] * blocks + local
            first, owner = jnp.int32(0), jnp.int32(-1)
            for d in range(docs):
                owner += (first <= block).astype(jnp.int32)
                first += counts_ref[d]
            keep = ids_ref[pl.ds(local, 1), :] == owner
            keep_ref[j : j + 1, :] = jnp.where(keep, 1.0, 0.0)
        doc = lax.broadcasted_iota(jnp.int32, (docs, LANES), 0)
        starts = jnp.zeros((docs, LANES), jnp.int32)
        broad = jnp.zeros((docs, LANES), jnp.int32)
        for d in range(docs):
            starts += jnp.where(doc > d, counts_ref[d], 0)
            broad += jnp.where(doc == d, counts_ref[d], 0)
        broad_ref[...] = broad.astype(jnp.float32)
        ends = starts + broad
        side, place, feat = where_ref[SIDE], where_ref[PLACE], where_ref[FEAT]
        for n in range(cols // LANES):
            col = lax.broadcasted_iota(jnp.int32, (docs, LANES), 1) + n * LANES
            at, cut = [], col
            for size in (units, mine, places, pairs, 2, 2):
                bits = size.bit_length() - 1
                at.append(cut & (size - 1))
                cut = lax.shift_right_logical(cut, bits)
            unit, j, k, x, y, c = at
            from_row = 2 * (place ^ k) + (side ^ y)
            which = from_row * blocks + (feat ^ (2 * x) ^ c) * mine + j
            holds = (starts <= which) & (which < ends)
            for u in range(units):
                part = jnp.where(holds & (unit == u), 1.0, 0.0).astype(jnp.bfloat16)
                member_ref[u * docs : (u + 1) * docs, n * LANES : (n + 1) * LANES] = part

    return pl.pallas_call(
        kernel,
        out_shape=[
            jax.ShapeDtypeStruct((units * docs, cols), jnp.bfloat16),
            jax.ShapeDtypeStruct((docs, LANES), jnp.float32),
            jax.ShapeDtypeStruct((mine, BLOCK), jnp.float32),
        ],
        in_specs=[SMEM, VMEM],
        out_specs=[VMEM, VMEM, VMEM],
        compiler_params=limit(4),
    )(counts, ids)


def begin(source_ref, base, held_ref, sems):
    tile = held_ref.shape[1] // sems.shape[0]
    copies = []
    for n in range(sems.shape[0]):
        at = pl.multiple_of(base + n * tile, tile)
        place = held_ref.at[:, pl.ds(n * tile, tile)]
        copies.append(pltpu.make_async_copy(source_ref.at[:, pl.ds(at, tile)], place, sems.at[n]))
    for copy in copies:
        copy.start()
    return copies


def quarter_of(side, turn):
    at = positions()
    return 2 * (at[SIDE] ^ side) + (at[TURN] ^ turn)


def fetch(inverse, side, turn):
    depth, cols = inverse.shape
    quarter = cols // 4

    def kernel(source_ref, out_ref, sems):
        for copy in begin(source_ref, quarter_of(side, turn) * quarter, out_ref, sems):
            copy.wait()

    return pl.pallas_call(
        kernel,
        out_shape=jax.ShapeDtypeStruct((depth, quarter), inverse.dtype),
        in_specs=[HBM],
        out_specs=VMEM,
        scratch_shapes=[pltpu.SemaphoreType.DMA((tiles(quarter),))],
        compiler_params=limit(6),
    )(in_hbm(inverse))


def tiles(quarter):
    return max(quarter // 512, 1)


def dense_body(left, grad_ref, diag_ref, ready_ref, copies, out_ref, side, turn):
    units = grad_ref.shape[0]
    quarter = out_ref.shape[1]
    steps = tiles(quarter)
    tile = quarter // steps
    ratio = lax.axis_size(ROWS) // lax.axis_size(FEATS)
    row, feat = lax.axis_index(ROWS), lax.axis_index(FEATS)
    start = jnp.where(row // ratio == feat, row % ratio * units, 1 << 20)
    for n in range(steps):
        col = n * tile
        if copies:
            copies[n].wait()
        total = jnp.dot(left, ready_ref[:, col : col + tile], preferred_element_type=jnp.float32)
        out_ref[:, col : col + tile] = total.astype(out_ref.dtype)
        for q in range(tile // LANES):
            unit = (quarter_of(side, turn) * quarter + col) // LANES + q - start

            @pl.when((unit >= 0) & (unit < units))
            def _():
                a = jnp.clip(unit, 0, units - 1)
                term = grad_ref[a].astype(jnp.float32) * diag_ref[pl.ds(a, 1), :]
                part = total[:, q * LANES : (q + 1) * LANES] + term
                cols = slice(col + q * LANES, col + (q + 1) * LANES)
                out_ref[:, cols] = part.astype(out_ref.dtype)


def joined(grad_ref):
    return jnp.concatenate([grad_ref[u] for u in range(grad_ref.shape[0])], axis=1)


def document_sums(member_ref, refs, first):
    each = refs[0].shape[0]
    blocks = jnp.concatenate([ref[...] for ref in refs], axis=0)
    part = member_ref[:, first * each : (first + len(refs)) * each]
    return jnp.dot(part, blocks, preferred_element_type=jnp.float32)


def early_sums(member, arrays):
    def kernel(member_ref, *refs):
        refs[-1][...] = document_sums(member_ref, refs[:-1], 0)

    return pl.pallas_call(
        kernel,
        out_shape=jax.ShapeDtypeStruct((member.shape[0], LANES), jnp.float32),
        in_specs=[VMEM] * (1 + len(arrays)),
        out_specs=VMEM,
        compiler_params=limit(8),
    )(member, *arrays)


OTHERS = ((1, 1), (1, 0), (0, 1))


def dense_others(member, counts, diag, ready, early, arrays, units):
    docs = counts.shape[0]
    first = (member.shape[1] // arrays[0].shape[0]) - len(arrays)
    quarter = ready[0].shape[1]

    def kernel(member_ref, counts_ref, diag_ref, early_ref, *refs):
        given, ready_refs = refs[: len(arrays)], refs[len(arrays) : len(arrays) + 3]
        grad_ref, outs = refs[-4], refs[-3:]
        summed = early_ref[...] + document_sums(member_ref, given, first)
        for u in range(units):
            mean = summed[u * docs : (u + 1) * docs] / counts_ref[...]
            grad_ref[u] = mean.astype(grad_ref.dtype)
        left = joined(grad_ref)
        for ready_ref, out_ref, (side, turn) in zip(ready_refs, outs, OTHERS):
            dense_body(left, grad_ref, diag_ref, ready_ref, None, out_ref, side, turn)

    shape = jax.ShapeDtypeStruct((docs, quarter), jnp.bfloat16)
    return pl.pallas_call(
        kernel,
        out_shape=[jax.ShapeDtypeStruct((units, docs, LANES), jnp.bfloat16)] + [shape] * 3,
        in_specs=[VMEM] * (7 + len(arrays)),
        out_specs=[VMEM] * 4,
        compiler_params=limit(8),
    )(member, counts, diag, early, *arrays, *ready)


def dense_own(docgrad, diag, inverse):
    depth, cols = inverse.shape
    quarter = cols // 4

    def kernel(grad_ref, diag_ref, source_ref, out_ref, held_ref, sems):
        copies = begin(source_ref, quarter_of(0, 0) * quarter, held_ref, sems)
        dense_body(joined(grad_ref), grad_ref, diag_ref, held_ref, copies, out_ref, 0, 0)

    return pl.pallas_call(
        kernel,
        out_shape=jax.ShapeDtypeStruct((docgrad.shape[1], quarter), jnp.float32),
        in_specs=[VMEM, VMEM, HBM],
        out_specs=VMEM,
        scratch_shapes=[
            pltpu.VMEM((depth, quarter), inverse.dtype),
            pltpu.SemaphoreType.DMA((tiles(quarter),)),
        ],
        compiler_params=limit(12),
    )(docgrad, diag, in_hbm(inverse))


def turned(train, other):
    count, cols = train.shape
    half = cols // 2
    steps = 4
    tile = half // steps

    def kernel(source_ref, out_ref, held_ref, sems):
        where_ref = positions()
        which = 1 - where_ref[SIDE] if other else where_ref[SIDE]
        copies = []
        for n in range(steps):
            at = pl.multiple_of(which * half + n * tile, tile)
            place = held_ref.at[:, pl.ds(n * tile, tile)]
            copies.append(pltpu.make_async_copy(source_ref.at[:, pl.ds(at, tile)], place, sems.at[n]))
        for copy in copies:
            copy.start()
        for n in range(steps):
            copies[n].wait()
            part = slice(n * tile, (n + 1) * tile)
            out_ref[part, :] = held_ref[:, part].T

    return pl.pallas_call(
        kernel,
        out_shape=jax.ShapeDtypeStruct((half, count), train.dtype),
        in_specs=[HBM],
        out_specs=VMEM,
        scratch_shapes=[
            pltpu.VMEM((count, half), train.dtype),
            pltpu.SemaphoreType.DMA((steps,)),
        ],
        compiler_params=limit(8),
    )(in_hbm(train))


def score_part(ref, train_ref, shift):
    quarter = ref.shape[1]
    at = pl.multiple_of((positions()[TURN] ^ shift) * quarter, quarter)
    return jnp.dot(ref[...], train_ref[pl.ds(at, quarter), :], preferred_element_type=jnp.float32)


def score_near(own, train):
    def kernel(own_ref, train_ref, out_ref):
        out_ref[...] = score_part(own_ref, train_ref, 0)

    return pl.pallas_call(
        kernel,
        out_shape=jax.ShapeDtypeStruct((own.shape[0], train.shape[1]), jnp.float32),
        in_specs=[VMEM] * 2,
        out_specs=VMEM,
        compiler_params=limit(4),
    )(own, train)


def score_beside(near, far, before, train):
    def kernel(near_ref, far_ref, before_ref, train_ref, out_ref):
        got = score_part(near_ref, train_ref, 0) + score_part(far_ref, train_ref, 1)
        out_ref[...] = before_ref[...] + got

    return pl.pallas_call(
        kernel,
        out_shape=jax.ShapeDtypeStruct(before.shape, jnp.float32),
        in_specs=[VMEM] * 4,
        out_specs=VMEM,
        compiler_params=limit(4),
    )(near, far, before, train)


def score_far(far, before, train, feats):
    docs, count = before.shape
    few = docs // feats
    shape = jax.ShapeDtypeStruct((few, count), jnp.float32)

    def kernel(far_ref, before_ref, train_ref, *refs):
        outs, all_ref = refs[:-1], refs[-1]
        all_ref[...] = before_ref[...] + score_part(far_ref, train_ref, 1)
        for m, ref in enumerate(outs):
            at = pl.multiple_of((positions()[FEAT] ^ m) * few, few)
            ref[...] = all_ref[pl.ds(at, few), :]

    return pl.pallas_call(
        kernel,
        out_shape=[shape] * feats,
        in_specs=[VMEM] * 3,
        out_specs=[VMEM] * feats,
        scratch_shapes=[pltpu.VMEM((docs, count), jnp.float32)],
        compiler_params=limit(4),
    )(far, before, train)


def per_device(
    acts,
    grads_out,
    proj_in,
    proj_out,
    doc_ids,
    block_counts,
    inverse_dense,
    inverse_diag,
    train_grads,
):
    tokens = acts.shape[0]
    rows = lax.axis_size(ROWS)
    feats = lax.axis_size(FEATS)
    feat = lax.axis_index(FEATS)
    width = proj_in.shape[1]
    part = tokens // feats
    mine = part // BLOCK
    blocks = tokens // BLOCK
    units = width // rows
    places = rows // 2
    f32, b16 = jnp.float32, jnp.bfloat16

    def across(left, right):
        both = jnp.dot(left, right, preferred_element_type=f32).reshape(feats, part, width)
        mask = 1
        while True:
            pairs = both.reshape(both.shape[0] // 2, 2, part, width)
            bit = (feat // mask) % 2
            sent = pick(pairs, 1 - bit, 1).astype(f32 if mask == 1 else b16)
            last = 2 * mask >= feats
            kept = pick(pairs, bit, 1)
            recv = swap(sent, FEATS, mask)
            mask *= 2
            if last:
                return kept[0], recv[0]
            both = kept + recv.astype(f32)

    kept_x, recv_x = across(acts, proj_in)
    kept_g, recv_g = across(grads_out, proj_out)

    ids = doc_ids.reshape(blocks, BLOCK)
    member, counts, keep = members(block_counts, ids, units, mine, places, feats // 2, blocks)
    arrays = block_sums(keep, kept_x, recv_x, kept_g, recv_g, places)
    arrays = [arrays[0]] + [swap(arrays[k], ROWS, 2 * k) for k in range(1, places)]
    own, other = deal(arrays, mine)

    def diagonal(x, mask):
        pairs = [
            (f * rows + r, (f ^ mask) * rows + (r ^ 1)) for f in range(feats) for r in range(rows)
        ]
        return lax.ppermute(x, (FEATS, ROWS), pairs)

    masks = range(2, feats, 2)
    got = [(0, m, diagonal(other, m)) for m in masks]
    got = got[::-1]
    crossed = {(1, m): x for _, m, x in got}
    crossed.update({(0, m): swap(own, FEATS, m) for m in masks})
    crossed[1, 0] = swap(other, ROWS, 1)
    crossed[0, 0] = own
    order = [(y, m) for y in (0, 1) for m in range(0, feats, 2)]
    parts = [crossed[at] for at in order]
    parts += [swap(crossed[y, m], FEATS, 1) for y, m in order]

    diag = inverse_diag.reshape(units, width)
    ready_both = fetch(inverse_dense, 1, 1)
    ready_side = fetch(inverse_dense, 1, 0)
    ready_turn = fetch(inverse_dense, 0, 1)
    ahead = len(parts) // 2 + 1
    early = early_sums(member, parts[:ahead])
    ready = (ready_both, ready_side, ready_turn)
    docgrad, *sent = dense_others(member, counts, diag, ready, early, parts[ahead:], units)
    part_both = swap(sent[0], ROWS, 3)
    part_side = swap(sent[1], ROWS, 1)
    part_turn = swap(sent[2], ROWS, 2)
    own = dense_own(docgrad, diag, inverse_dense)
    own = own + part_both.astype(f32) + part_side.astype(f32) + part_turn.astype(f32)
    mask = 4
    while mask < rows:
        own = own + swap(own.astype(b16), ROWS, mask).astype(f32)
        mask *= 2
    own = own.astype(b16)
    train_near = turned(train_grads, False)
    train_far = turned(train_grads, True)
    own_both = swap(own, ROWS, 3)
    own_side = swap(own, ROWS, 1)
    own_turn = swap(own, ROWS, 2)
    before = score_near(own, train_near)
    before = score_beside(own_side, own_both, before, train_far)

    pieces = score_far(own_turn, before, train_near, feats)
    arrived = [swap(pieces[m], FEATS, m) for m in range(feats - 1, 0, -1)]
    scores = pieces[0]
    for piece in arrived:
        scores = scores + piece
    return scores


def solution(mesh):
    in_specs = (
        P(ROWS, FEATS),
        P(ROWS, FEATS),
        P(FEATS, None),
        P(FEATS, None),
        P(ROWS),
        P(),
        P(ROWS, FEATS),
        P(ROWS),
        P(ROWS, FEATS),
    )
    out_specs = P(FEATS, ROWS)
    return jax.shard_map(per_device, mesh=mesh, in_specs=in_specs, out_specs=out_specs, check_vma=False)
```

```python
import jax
import jax.numpy as jnp
from jax import lax
from jax.experimental import pallas as pl
from jax.experimental.pallas import tpu as pltpu
from jax.sharding import PartitionSpec as P


BLOCK = 128
LANES = 128
SMEM = pl.BlockSpec(memory_space=pltpu.SMEM)
VMEM = pl.BlockSpec(memory_space=pltpu.VMEM)
HBM = pl.BlockSpec(memory_space=pltpu.HBM)
ROWS, FEATS = "rows", "feat"
_, FEAT, SIDE, TURN, PLACE, ROW = range(6)


def positions():
    row, feat = lax.axis_index(ROWS), lax.axis_index(FEATS)
    return feat & 1, feat, row & 1, (row >> 1) & 1, row >> 1, row


def swap(x, axis, mask):
    count = lax.axis_size(axis)
    return lax.ppermute(x, axis, [(i, i ^ mask) for i in range(count)])


def pick(x, index, axis=0):
    return lax.dynamic_index_in_dim(x, index, axis, keepdims=False)


def in_hbm(x):
    return pltpu.with_memory_space_constraint(x, pltpu.HBM)


def limit(mib):
    return pltpu.CompilerParams(vmem_limit_bytes=mib << 20)


def sums_kernel(keep_ref, kx_ref, rx_ref, kg_ref, rg_ref, *refs):
    outs, sums_ref = refs[:-1], refs[-1]
    mine = sums_ref.shape[0]
    where_ref = positions()
    xin = (kx_ref[...] + rx_ref[...].astype(jnp.float32)).astype(jnp.bfloat16)
    gout = (kg_ref[...] + rg_ref[...].astype(jnp.float32)).astype(jnp.bfloat16)
    for j in range(mine):
        part = slice(j * BLOCK, (j + 1) * BLOCK)
        flipped = gout[part].astype(jnp.float32).T
        masked = jnp.where(keep_ref[j : j + 1, :] > 0.0, flipped, 0.0).astype(jnp.bfloat16)
        sums_ref[j] = jnp.dot(masked, xin[part], preferred_element_type=jnp.float32)
    few = outs[0].shape[0] // mine
    for k, out_ref in enumerate(outs):
        at = pl.multiple_of((where_ref[PLACE] ^ k) * few, few)
        for j in range(mine):
            piece = sums_ref[j, pl.ds(at, few), :]
            out_ref[j * few : (j + 1) * few] = piece.astype(out_ref.dtype)


def block_sums(keep, kept_x, recv_x, kept_g, recv_g, places):
    part, width = kept_x.shape
    mine = part // BLOCK
    few = width // places
    shape = jax.ShapeDtypeStruct((mine * few, width), jnp.bfloat16)
    return pl.pallas_call(
        sums_kernel,
        out_shape=[shape] * places,
        in_specs=[VMEM] * 5,
        out_specs=[VMEM] * places,
        scratch_shapes=[pltpu.VMEM((mine, width, width), jnp.float32)],
        compiler_params=limit(8),
    )(keep, kept_x, recv_x, kept_g, recv_g)


def deal(arrays, mine):
    rows, width = arrays[0].shape
    shape = jax.ShapeDtypeStruct((len(arrays) * rows // 2, width), arrays[0].dtype)

    def kernel(*refs):
        where_ref = positions()
        own_ref, other_ref = refs[-2:]
        first = where_ref[SIDE] == 0
        few = rows // mine
        half = few // 2
        for k, ref in enumerate(refs[:-2]):
            got = ref[...].astype(jnp.float32)
            for j in range(mine):
                low, high = got[j * few : j * few + half], got[j * few + half : (j + 1) * few]
                at = slice((k * mine + j) * half, (k * mine + j + 1) * half)
                own_ref[at] = jnp.where(first, low, high).astype(own_ref.dtype)
                other_ref[at] = jnp.where(first, high, low).astype(own_ref.dtype)

    return pl.pallas_call(
        kernel,
        out_shape=[shape, shape],
        in_specs=[VMEM] * len(arrays),
        out_specs=[VMEM, VMEM],
        compiler_params=limit(4),
    )(*arrays)


def members(counts, ids, units, mine, places, pairs, blocks):
    docs = counts.shape[0]
    cols = units * mine * places * pairs * 4

    def kernel(counts_ref, ids_ref, member_ref, broad_ref, keep_ref):
        where_ref = positions()
        for j in range(mine):
            local = where_ref[FEAT] * mine + j
            block = where_ref[ROW] * blocks + local
            first, owner = jnp.int32(0), jnp.int32(-1)
            for d in range(docs):
                owner += (first <= block).astype(jnp.int32)
                first += counts_ref[d]
            keep = ids_ref[pl.ds(local, 1), :] == owner
            keep_ref[j : j + 1, :] = jnp.where(keep, 1.0, 0.0)
        doc = lax.broadcasted_iota(jnp.int32, (docs, LANES), 0)
        starts = jnp.zeros((docs, LANES), jnp.int32)
        broad = jnp.zeros((docs, LANES), jnp.int32)
        for d in range(docs):
            starts += jnp.where(doc > d, counts_ref[d], 0)
            broad += jnp.where(doc == d, counts_ref[d], 0)
        broad_ref[...] = broad.astype(jnp.float32)
        ends = starts + broad
        side, place, feat = where_ref[SIDE], where_ref[PLACE], where_ref[FEAT]
        for n in range(cols // LANES):
            col = lax.broadcasted_iota(jnp.int32, (docs, LANES), 1) + n * LANES
            at, cut = [], col
            for size in (units, mine, places, pairs, 2, 2):
                bits = size.bit_length() - 1
                at.append(cut & (size - 1))
                cut = lax.shift_right_logical(cut, bits)
            unit, j, k, x, y, c = at
            from_row = 2 * (place ^ k) + (side ^ y)
            which = from_row * blocks + (feat ^ (2 * x) ^ c) * mine + j
            holds = (starts <= which) & (which < ends)
            for u in range(units):
                part = jnp.where(holds & (unit == u), 1.0, 0.0).astype(jnp.bfloat16)
                member_ref[u * docs : (u + 1) * docs, n * LANES : (n + 1) * LANES] = part

    return pl.pallas_call(
        kernel,
        out_shape=[
            jax.ShapeDtypeStruct((units * docs, cols), jnp.bfloat16),
            jax.ShapeDtypeStruct((docs, LANES), jnp.float32),
            jax.ShapeDtypeStruct((mine, BLOCK), jnp.float32),
        ],
        in_specs=[SMEM, VMEM],
        out_specs=[VMEM, VMEM, VMEM],
        compiler_params=limit(4),
    )(counts, ids)


def begin(source_ref, base, held_ref, sems):
    tile = held_ref.shape[1] // sems.shape[0]
    copies = []
    for n in range(sems.shape[0]):
        at = pl.multiple_of(base + n * tile, tile)
        place = held_ref.at[:, pl.ds(n * tile, tile)]
        copies.append(pltpu.make_async_copy(source_ref.at[:, pl.ds(at, tile)], place, sems.at[n]))
    for copy in copies:
        copy.start()
    return copies


def quarter_of(side, turn):
    at = positions()
    return 2 * (at[SIDE] ^ side) + (at[TURN] ^ turn)


def fetch(inverse, side, turn):
    depth, cols = inverse.shape
    quarter = cols // 4

    def kernel(source_ref, out_ref, sems):
        for copy in begin(source_ref, quarter_of(side, turn) * quarter, out_ref, sems):
            copy.wait()

    return pl.pallas_call(
        kernel,
        out_shape=jax.ShapeDtypeStruct((depth, quarter), inverse.dtype),
        in_specs=[HBM],
        out_specs=VMEM,
        scratch_shapes=[pltpu.SemaphoreType.DMA((tiles(quarter),))],
        compiler_params=limit(6),
    )(in_hbm(inverse))


def tiles(quarter):
    return max(quarter // 512, 1)


def dense_body(left, grad_ref, diag_ref, ready_ref, copies, out_ref, side, turn):
    units = grad_ref.shape[0]
    quarter = out_ref.shape[1]
    steps = tiles(quarter)
    tile = quarter // steps
    ratio = lax.axis_size(ROWS) // lax.axis_size(FEATS)
    row, feat = lax.axis_index(ROWS), lax.axis_index(FEATS)
    start = jnp.where(row // ratio == feat, row % ratio * units, 1 << 20)
    for n in range(steps):
        col = n * tile
        if copies:
            copies[n].wait()
        total = jnp.dot(left, ready_ref[:, col : col + tile], preferred_element_type=jnp.float32)
        out_ref[:, col : col + tile] = total.astype(out_ref.dtype)
        for q in range(tile // LANES):
            unit = (quarter_of(side, turn) * quarter + col) // LANES + q - start

            @pl.when((unit >= 0) & (unit < units))
            def _():
                a = jnp.clip(unit, 0, units - 1)
                term = grad_ref[a].astype(jnp.float32) * diag_ref[pl.ds(a, 1), :]
                part = total[:, q * LANES : (q + 1) * LANES] + term
                cols = slice(col + q * LANES, col + (q + 1) * LANES)
                out_ref[:, cols] = part.astype(out_ref.dtype)


def joined(grad_ref):
    return jnp.concatenate([grad_ref[u] for u in range(grad_ref.shape[0])], axis=1)


def document_sums(member_ref, refs, first):
    each = refs[0].shape[0]
    blocks = jnp.concatenate([ref[...] for ref in refs], axis=0)
    part = member_ref[:, first * each : (first + len(refs)) * each]
    return jnp.dot(part, blocks, preferred_element_type=jnp.float32)


def early_sums(member, arrays):
    def kernel(member_ref, *refs):
        refs[-1][...] = document_sums(member_ref, refs[:-1], 0)

    return pl.pallas_call(
        kernel,
        out_shape=jax.ShapeDtypeStruct((member.shape[0], LANES), jnp.float32),
        in_specs=[VMEM] * (1 + len(arrays)),
        out_specs=VMEM,
        compiler_params=limit(8),
    )(member, *arrays)


def dense_first(member, counts, diag, ready, early, arrays, units, side, turn):
    docs = counts.shape[0]
    first = (member.shape[1] // arrays[0].shape[0]) - len(arrays)

    def kernel(member_ref, counts_ref, diag_ref, ready_ref, early_ref, *refs):
        given, (out_ref, grad_ref) = refs[:-2], refs[-2:]
        summed = early_ref[...] + document_sums(member_ref, given, first)
        for u in range(units):
            mean = summed[u * docs : (u + 1) * docs] / counts_ref[...]
            grad_ref[u] = mean.astype(grad_ref.dtype)
        dense_body(joined(grad_ref), grad_ref, diag_ref, ready_ref, None, out_ref, side, turn)

    return pl.pallas_call(
        kernel,
        out_shape=[
            jax.ShapeDtypeStruct((docs, ready.shape[1]), jnp.bfloat16),
            jax.ShapeDtypeStruct((units, docs, LANES), jnp.bfloat16),
        ],
        in_specs=[VMEM] * (5 + len(arrays)),
        out_specs=[VMEM, VMEM],
        compiler_params=limit(8),
    )(member, counts, diag, ready, early, *arrays)


def dense_ready(docgrad, diag, ready, side, turn):
    def kernel(grad_ref, diag_ref, ready_ref, out_ref):
        dense_body(joined(grad_ref), grad_ref, diag_ref, ready_ref, None, out_ref, side, turn)

    return pl.pallas_call(
        kernel,
        out_shape=jax.ShapeDtypeStruct((docgrad.shape[1], ready.shape[1]), jnp.bfloat16),
        in_specs=[VMEM] * 3,
        out_specs=VMEM,
        compiler_params=limit(8),
    )(docgrad, diag, ready)


def dense_own(docgrad, diag, inverse):
    depth, cols = inverse.shape
    quarter = cols // 4

    def kernel(grad_ref, diag_ref, source_ref, out_ref, held_ref, sems):
        copies = begin(source_ref, quarter_of(0, 0) * quarter, held_ref, sems)
        dense_body(joined(grad_ref), grad_ref, diag_ref, held_ref, copies, out_ref, 0, 0)

    return pl.pallas_call(
        kernel,
        out_shape=jax.ShapeDtypeStruct((docgrad.shape[1], quarter), jnp.float32),
        in_specs=[VMEM, VMEM, HBM],
        out_specs=VMEM,
        scratch_shapes=[
            pltpu.VMEM((depth, quarter), inverse.dtype),
            pltpu.SemaphoreType.DMA((tiles(quarter),)),
        ],
        compiler_params=limit(12),
    )(docgrad, diag, in_hbm(inverse))


def turned(train, other):
    count, cols = train.shape
    half = cols // 2
    steps = 4
    tile = half // steps

    def kernel(source_ref, out_ref, held_ref, sems):
        where_ref = positions()
        which = 1 - where_ref[SIDE] if other else where_ref[SIDE]
        copies = []
        for n in range(steps):
            at = pl.multiple_of(which * half + n * tile, tile)
            place = held_ref.at[:, pl.ds(n * tile, tile)]
            copies.append(pltpu.make_async_copy(source_ref.at[:, pl.ds(at, tile)], place, sems.at[n]))
        for copy in copies:
            copy.start()
        for n in range(steps):
            copies[n].wait()
            part = slice(n * tile, (n + 1) * tile)
            out_ref[part, :] = held_ref[:, part].T

    return pl.pallas_call(
        kernel,
        out_shape=jax.ShapeDtypeStruct((half, count), train.dtype),
        in_specs=[HBM],
        out_specs=VMEM,
        scratch_shapes=[
            pltpu.VMEM((count, half), train.dtype),
            pltpu.SemaphoreType.DMA((steps,)),
        ],
        compiler_params=limit(8),
    )(in_hbm(train))


def score_part(ref, train_ref, shift):
    quarter = ref.shape[1]
    at = pl.multiple_of((positions()[TURN] ^ shift) * quarter, quarter)
    return jnp.dot(ref[...], train_ref[pl.ds(at, quarter), :], preferred_element_type=jnp.float32)


def score_near(own, train):
    def kernel(own_ref, train_ref, out_ref):
        out_ref[...] = score_part(own_ref, train_ref, 0)

    return pl.pallas_call(
        kernel,
        out_shape=jax.ShapeDtypeStruct((own.shape[0], train.shape[1]), jnp.float32),
        in_specs=[VMEM] * 2,
        out_specs=VMEM,
        compiler_params=limit(4),
    )(own, train)


def score_beside(near, far, before, train):
    def kernel(near_ref, far_ref, before_ref, train_ref, out_ref):
        got = score_part(near_ref, train_ref, 0) + score_part(far_ref, train_ref, 1)
        out_ref[...] = before_ref[...] + got

    return pl.pallas_call(
        kernel,
        out_shape=jax.ShapeDtypeStruct(before.shape, jnp.float32),
        in_specs=[VMEM] * 4,
        out_specs=VMEM,
        compiler_params=limit(4),
    )(near, far, before, train)


def score_far(far, before, train, feats):
    docs, count = before.shape
    few = docs // feats
    shape = jax.ShapeDtypeStruct((few, count), jnp.float32)

    def kernel(far_ref, before_ref, train_ref, *refs):
        outs, all_ref = refs[:-1], refs[-1]
        all_ref[...] = before_ref[...] + score_part(far_ref, train_ref, 1)
        for m, ref in enumerate(outs):
            at = pl.multiple_of((positions()[FEAT] ^ m) * few, few)
            ref[...] = all_ref[pl.ds(at, few), :]

    return pl.pallas_call(
        kernel,
        out_shape=[shape] * feats,
        in_specs=[VMEM] * 3,
        out_specs=[VMEM] * feats,
        scratch_shapes=[pltpu.VMEM((docs, count), jnp.float32)],
        compiler_params=limit(4),
    )(far, before, train)


def per_device(
    acts,
    grads_out,
    proj_in,
    proj_out,
    doc_ids,
    block_counts,
    inverse_dense,
    inverse_diag,
    train_grads,
):
    tokens = acts.shape[0]
    rows = lax.axis_size(ROWS)
    feats = lax.axis_size(FEATS)
    feat = lax.axis_index(FEATS)
    width = proj_in.shape[1]
    part = tokens // feats
    mine = part // BLOCK
    blocks = tokens // BLOCK
    units = width // rows
    places = rows // 2
    f32, b16 = jnp.float32, jnp.bfloat16

    def across(left, right):
        both = jnp.dot(left, right, preferred_element_type=f32).reshape(feats, part, width)
        mask = 1
        while True:
            pairs = both.reshape(both.shape[0] // 2, 2, part, width)
            bit = (feat // mask) % 2
            sent = pick(pairs, 1 - bit, 1).astype(f32 if mask == 1 else b16)
            last = 2 * mask >= feats
            kept = pick(pairs, bit, 1)
            recv = swap(sent, FEATS, mask)
            mask *= 2
            if last:
                return kept[0], recv[0]
            both = kept + recv.astype(f32)

    kept_x, recv_x = across(acts, proj_in)
    kept_g, recv_g = across(grads_out, proj_out)

    ids = doc_ids.reshape(blocks, BLOCK)
    member, counts, keep = members(block_counts, ids, units, mine, places, feats // 2, blocks)
    arrays = block_sums(keep, kept_x, recv_x, kept_g, recv_g, places)
    arrays = [arrays[0]] + [swap(arrays[k], ROWS, 2 * k) for k in range(1, places)]
    own, other = deal(arrays, mine)

    def diagonal(x, mask):
        pairs = [
            (f * rows + r, (f ^ mask) * rows + (r ^ 1)) for f in range(feats) for r in range(rows)
        ]
        return lax.ppermute(x, (FEATS, ROWS), pairs)

    masks = range(2, feats, 2)
    got = [(0, m, diagonal(other, m)) for m in masks]
    got = got[::-1]
    crossed = {(1, m): x for _, m, x in got}
    crossed.update({(0, m): swap(own, FEATS, m) for m in masks})
    crossed[1, 0] = swap(other, ROWS, 1)
    crossed[0, 0] = own
    order = [(y, m) for y in (0, 1) for m in range(0, feats, 2)]
    parts = [crossed[at] for at in order]
    parts += [swap(crossed[y, m], FEATS, 1) for y, m in order]

    diag = inverse_diag.reshape(units, width)
    ready_both = fetch(inverse_dense, 1, 1)
    ready_side = fetch(inverse_dense, 1, 0)
    ready_turn = fetch(inverse_dense, 0, 1)
    ahead = len(parts) // 2 + 1
    early = early_sums(member, parts[:ahead])
    part, docgrad = dense_first(
        member, counts, diag, ready_both, early, parts[ahead:], units, 1, 1
    )
    part_both = swap(part, ROWS, 3)
    part = dense_ready(docgrad, diag, ready_turn, 0, 1)
    part_turn = swap(part, ROWS, 2)
    part = dense_ready(docgrad, diag, ready_side, 1, 0)
    part_side = swap(part, ROWS, 1)
    own = dense_own(docgrad, diag, inverse_dense)
    own = own + part_both.astype(f32) + part_side.astype(f32) + part_turn.astype(f32)
    mask = 4
    while mask < rows:
        own = own + swap(own.astype(b16), ROWS, mask).astype(f32)
        mask *= 2
    own = own.astype(b16)
    train_near = turned(train_grads, False)
    train_far = turned(train_grads, True)
    own_both = swap(own, ROWS, 3)
    own_side = swap(own, ROWS, 1)
    own_turn = swap(own, ROWS, 2)
    before = score_near(own, train_near)
    before = score_beside(own_side, own_both, before, train_far)

    pieces = score_far(own_turn, before, train_near, feats)
    arrived = [swap(pieces[m], FEATS, m) for m in range(feats - 1, 0, -1)]
    scores = pieces[0]
    for piece in arrived:
        scores = scores + piece
    return scores


def solution(mesh):
    in_specs = (
        P(ROWS, FEATS),
        P(ROWS, FEATS),
        P(FEATS, None),
        P(FEATS, None),
        P(ROWS),
        P(),
        P(ROWS, FEATS),
        P(ROWS),
        P(ROWS, FEATS),
    )
    out_specs = P(FEATS, ROWS)
    return jax.shard_map(per_device, mesh=mesh, in_specs=in_specs, out_specs=out_specs, check_vma=False)
```
